32 devices in a mesh: parts: 2 (over y), pol: 4 (over z), scen: 2 (over x), fund: 2 (over core).
Axes of the slice: x: 2, y: 2, z: 4, core: 2. Of those that a mesh axis runs over, the one named last changes fastest.
Arguments:
- count_init: float32 [32768], P(('pol', 'fund')), may hold values from 0.5 to 2
- value_init: float32 [32768], P(('pol', 'fund')), may hold values from 0.5 to 4
- durations: int32 [32768], P(('pol', 'fund')), may hold values from 0 to 119
- products: int32 [32768], P(('pol', 'fund')), may hold values from 0 to 7
- policy_fund: int32 [32768], P(('pol', 'fund')), may hold values from 0 to 119, as said below
- lapse_base: float32 [8], replicated, may hold values from 0.05 to 0.1
- lapse_sens: float32 [8], replicated, may hold values from 6 to 10
- fee_rate: float32 [8], replicated, may hold values from 0.002 to 0.02
- fund_share: float32 [120], replicated, may hold values from 0.3 to 1
- bond_flows: float32 [16384, 120], P(('pol', 'fund')), may hold values from 0.05 to 1
- bond_fund: int32 [16384], P(('pol', 'fund')), may hold values from 0 to 119, as said below
- holdings: float32 [16384], P(('pol', 'fund')), may hold values from 0.037 to 0.3
- scen_rates: float32 [3, 120, 512], P(None, None, ('parts', 'scen')), parts along dimension 2, may hold values from 0 to 0.12
Outputs:
- credited: float32 [3, 120, 512], P(None, None, ('parts', 'scen')), parts along dimension 2
- reserve: float32 [512, 32768], P(('parts', 'scen'), ('pol', 'fund')), parts along dimension 0
The draws below stay inside these ranges and needn't reach their ends.
There are 2 independent parts, one for each index of `parts`. The reference program is written for one: setup_inputs(seed, part) draws one part's arguments, and reference() takes and returns one part's arrays. A program takes and returns all parts, laid end to end along the dimension named above; an argument that names none is the same for every part. Nothing has to cross between parts.
Inputs may be any that keep to these rules, and one draw needn't show every extreme that they name: `policy_fund`: every fund number appears at least once. `bond_fund`: every fund number appears at least once.
All inputs are finite; a program needn't handle non-finite values.
Results may differ from the reference program's by a relative error of at most 0.0003.
Values sent between devices are 32-bit elements; how exact they have to be, the bound alone decides.
A program may use at most 64 MiB of HBM per device.

```python
import math
import jax
import jax.numpy as jnp
from jax import lax

FUNDS = 120
TENORS = 120
PRODUCTS = 8
MONTHS = 3
S_DEV = 128
POLICIES = 32768
BONDS = 16384
SCEN = 256


def covering(key, total_count):
    spread = jax.random.permutation(jax.random.fold_in(key, 17), FUNDS)
    others = jax.random.randint(jax.random.fold_in(key, 29), (total_count,), 0, FUNDS)
    positions = jnp.arange(total_count)
    picked = spread[jnp.minimum(positions, FUNDS - 1)]
    return jnp.where(positions < FUNDS, picked, others).astype(jnp.int32)


def draw_policy_fund(key, part):
    return covering(jax.random.fold_in(key, 5), POLICIES)


def draw_bond_fund(key, part):
    return covering(jax.random.fold_in(key, 7), BONDS)


def with_ends(result, own_key, smallest, top_value):
    extent = result.shape
    place = [jax.random.randint(jax.random.fold_in(own_key, axis), (), 0, extent[axis]) for axis in range(len(extent))]
    result = result.at[tuple(place)].set(smallest)
    longest = extent.index(max(extent))
    place[longest] = (place[longest] + 1) % extent[longest]
    return result.at[tuple(place)].set(top_value)


def levels(key, dims, pieces, smallest, largest):
    loudness, own = 1.0, jax.random.fold_in(key, 6)
    for position, parts in pieces:
        steps = jnp.exp(jax.random.uniform(jax.random.fold_in(own, position), (parts,), jnp.float32, smallest / len(pieces), largest / len(pieces)))
        loudness = loudness * jnp.repeat(steps, dims[position] // parts).reshape([-1 if axis == position else 1 for axis in range(len(dims))])
    return loudness


def setup_inputs(seed: int = 0, part: int = 0) -> dict:
    key_of = jax.random.split(jax.random.key(seed), 14)
    part_keys = jax.random.split(jax.random.fold_in(key_of[13], part), 14)
    count_init = jnp.clip(jnp.exp(math.log(2.0) - 1.3862944 * jax.random.uniform(key_of[0], (POLICIES,), jnp.float32) ** levels(key_of[0], (POLICIES,), ((0, 8),), -0.2, 0.2)), 0.5, 2.0)
    value_init = jnp.clip(jnp.exp(math.log(4.0) - 2.0794415 * jax.random.uniform(key_of[1], (POLICIES,), jnp.float32) ** levels(key_of[1], (POLICIES,), ((0, 8),), -0.2, 0.2)), 0.5, 4.0)
    durations = with_ends(jax.random.randint(key_of[2], (POLICIES,), 0, 120), jax.random.fold_in(key_of[2], 1), 0, 119).astype(jnp.int32)
    products = with_ends(jax.random.randint(key_of[3], (POLICIES,), 0, PRODUCTS), jax.random.fold_in(key_of[3], 1), 0, PRODUCTS - 1).astype(jnp.int32)
    policy_fund = draw_policy_fund(jax.random.fold_in(key_of[13], 71), part)
    lapse_base = jnp.clip(jnp.exp(jax.random.uniform(key_of[5], (PRODUCTS,), jnp.float32, math.log(0.05), math.log(0.1))), 0.05, 0.1)
    lapse_sens = jnp.clip(jax.random.uniform(key_of[6], (PRODUCTS,), jnp.float32, 6.0, 10.0), 6.0, 10.0)
    fee_rate = jnp.clip(jnp.exp(jax.random.uniform(key_of[7], (PRODUCTS,), jnp.float32, math.log(0.002), math.log(0.02))), 0.002, 0.02)
    fund_share = jnp.clip(jnp.exp(jax.random.uniform(key_of[8], (FUNDS,), jnp.float32, math.log(0.3), math.log(1.0))), 0.3, 1.0)
    bond_flows = jnp.clip(jnp.exp(math.log(1.0) - 2.9957323 * jax.random.uniform(key_of[9], (BONDS, TENORS), jnp.float32) ** levels(key_of[9], (BONDS, TENORS), ((0, 8),), -0.2, 0.2)), 0.05, 1.0)
    bond_fund = draw_bond_fund(jax.random.fold_in(key_of[13], 71), part)
    holdings = jnp.clip(jnp.exp(math.log(0.3) - 2.0928646 * jax.random.uniform(key_of[11], (BONDS,), jnp.float32) ** levels(key_of[11], (BONDS,), ((0, 8),), -0.2, 0.2)), 0.037, 0.3)
    scen_rates = jnp.clip(0.12 * jax.random.uniform(part_keys[12], (MONTHS, TENORS, SCEN), jnp.float32) ** levels(part_keys[12], (MONTHS, TENORS, SCEN), ((2, 2),), -0.2, 0.2), 0.0, 0.12)
    return dict(count_init=count_init, value_init=value_init, durations=durations, products=products, policy_fund=policy_fund, lapse_base=lapse_base, lapse_sens=lapse_sens, fee_rate=fee_rate, fund_share=fund_share, bond_flows=bond_flows, bond_fund=bond_fund, holdings=holdings, scen_rates=scen_rates)


surrender_end = 84
highest = lax.Precision.HIGHEST


def project_block(block_rates, count_init, value_init, durations, products, policy_fund, lapse_base, lapse_sens, fee_rate, fund_share, bond_flows, bond_fund, holdings):
    tenor_years = (jnp.arange(TENORS).astype(jnp.float32) + 1.0) / 12.0
    width_scen = block_rates.shape[2]
    lapse_pol = lapse_base[products]
    sens_pol = lapse_sens[products]
    fee_pol = fee_rate[products]
    in_force = jnp.broadcast_to(count_init[None, :], (width_scen, POLICIES))
    account = jnp.broadcast_to(value_init[None, :], (width_scen, POLICIES))
    credited_list = []
    for month_idx in range(MONTHS):
        discount = jnp.exp(-block_rates[month_idx] * tenor_years[:, None])
        bond_values = jnp.dot(bond_flows, discount, precision=highest, preferred_element_type=jnp.float32)
        assets = jax.ops.segment_sum(bond_values * holdings[:, None], bond_fund, num_segments=FUNDS)
        reserve = in_force * account
        liabilities = jax.ops.segment_sum(reserve.T, policy_fund, num_segments=FUNDS)
        credited = fund_share[:, None] * jnp.log(assets / liabilities)
        credit_pol = credited[policy_fund].T
        market = block_rates[month_idx, TENORS - 1]
        later_mult = jnp.where(durations + month_idx >= surrender_end, 2.0, 1.0)
        lapse_now = (lapse_pol * later_mult)[None, :] * jnp.exp(sens_pol[None, :] * (market[:, None] - credit_pol))
        in_force = in_force * jnp.exp(-lapse_now)
        account = account * jnp.exp(credit_pol / 12.0 - fee_pol[None, :])
        credited_list.append(credited)
    return jnp.stack(credited_list), in_force * account


def reference(count_init, value_init, durations, products, policy_fund, lapse_base, lapse_sens, fee_rate, fund_share, bond_flows, bond_fund, holdings, scen_rates):
    block_count = SCEN // S_DEV
    blocked = scen_rates.reshape(MONTHS, TENORS, block_count, S_DEV).transpose(2, 0, 1, 3)

    def one_block(block_rates):
        return project_block(block_rates, count_init, value_init, durations, products, policy_fund, lapse_base, lapse_sens, fee_rate, fund_share, bond_flows, bond_fund, holdings)

    credited_blocks, reserve_blocks = lax.map(one_block, blocked)
    credited = credited_blocks.transpose(1, 2, 0, 3).reshape(MONTHS, FUNDS, SCEN)
    reserve = reserve_blocks.reshape(SCEN, POLICIES)
    return (credited, reserve)
```

```python
import functools

import jax
import jax.numpy as jnp
from jax import lax
from jax.experimental import pallas as pl
from jax.experimental.pallas import tpu as pltpu
from jax.sharding import PartitionSpec as P

surrender_end = 84
lanes = 128
log2_e = 1.4426950408889634
f32, bf16 = jnp.float32, jnp.bfloat16
contract_cols = (((1,), (1,)), ((), ()))


def round_up(value, unit):
    return -(-value // unit) * unit


def split(value):
    high = value.astype(bf16)
    return high, (value - high.astype(f32)).astype(bf16)


def dot(left, right):
    return jnp.dot(left, right, preferred_element_type=f32)


def dot_cols(left, right):
    return lax.dot_general(left, right, contract_cols, preferred_element_type=f32)


def onehot(ids_row, values, row_count):
    shape = (16, ids_row.shape[1])
    kind = bf16 if row_count <= 256 else f32
    ids = jnp.broadcast_to(ids_row.astype(f32), shape).astype(kind)
    rows = lax.broadcasted_iota(jnp.int32, shape, 0).astype(f32)
    values = [jnp.broadcast_to(v, shape).astype(bf16) for v in values]
    masks = [ids == (rows + float(g)).astype(kind) for g in range(0, row_count, 16)]
    zero = jnp.zeros(shape, bf16)
    return [jnp.concatenate([jnp.where(m, v, zero) for m in masks], axis=0) for v in values]


def split_row(row):
    high = row.astype(bf16).astype(f32)
    return high, row - high


def gather_kernel(
    group,
    kinds,
    funds,
    bfund_hbm,
    hold_hbm,
    flows_hbm,
    pfund_hbm,
    count_hbm,
    value_hbm,
    dur_hbm,
    prod_hbm,
    base_hbm,
    sens_hbm,
    fee_hbm,
    share_hbm,
    rates_hbm,
    out_ref,
    hot_ref,
    rows_ref,
    disc_ref,
    market_ref,
    kind_ref,
    share_ref,
    bfund_ref,
    hold_ref,
    flows_ref,
    pfund_ref,
    count_ref,
    value_ref,
    dur_ref,
    prod_ref,
    base_ref,
    sens_ref,
    fee_ref,
    rates_ref,
    in_sems,
    part_buf,
    recv_buf,
    sum_buf,
    send_a,
    recv_a,
    send_b,
    recv_b,
):
    pol_devs, fund_devs = group
    n = pol_devs * fund_devs
    pairs = (
        (bfund_hbm, bfund_ref),
        (hold_hbm, hold_ref),
        (flows_hbm, flows_ref),
        (pfund_hbm, pfund_ref),
        (count_hbm, count_ref),
        (value_hbm, value_ref),
        (dur_hbm, dur_ref),
        (prod_hbm, prod_ref),
        (base_hbm, base_ref),
        (sens_hbm, sens_ref),
        (fee_hbm, fee_ref),
        (share_hbm, share_ref),
        (rates_hbm, rates_ref),
    )
    loads = [
        pltpu.make_async_copy(src, dst, in_sems.at[i]) for i, (src, dst) in enumerate(pairs)
    ]
    for load in loads:
        load.start()
    me = lax.axis_index("pol") * fund_devs + lax.axis_index("fund")

    def peer_of(step):
        peer = lax.rem(me + step, n)
        return peer, {"pol": peer // fund_devs, "fund": lax.rem(peer, fund_devs)}

    barrier = pltpu.get_barrier_semaphore()
    for step in range(1, n):
        pl.semaphore_signal(
            barrier, inc=1, device_id=peer_of(step)[1], device_id_type=pl.DeviceIdType.MESH
        )

    months, tenors, scen = rates_ref.shape
    wide = part_buf.shape[2]
    chunk = part_buf.shape[1]
    part_buf[...] = jnp.zeros_like(part_buf)

    for load in loads[3:8]:
        load.wait()
    worth = count_ref[...] * value_ref[...]
    late = jnp.clip(dur_ref[...] - (surrender_end - (months - 1)), 0, months - 1)
    kind = late * kinds + prod_ref[...]
    classed = onehot(kind, split_row(worth), round_up(months * kinds, 16))
    (pol_hot,) = onehot(pfund_ref[...], [jnp.ones(worth.shape, f32)], wide)
    hot_ref[...] = pol_hot
    sides = dot_cols(jnp.concatenate(classed, axis=0), pol_hot)
    half = sides.shape[0] // 2
    classes = (sides[:half] + sides[half:])[: months * kinds]

    for load in loads[:3]:
        load.wait()
    flows = flows_ref[...]
    if wide > tenors:
        flows = jnp.concatenate(
            [flows, jnp.zeros((wide - tenors, flows.shape[1]), f32)], axis=0
        )
    held = jnp.concatenate(onehot(bfund_ref[...], split_row(hold_ref[...]), wide), axis=0)
    quads = dot_cols(held, jnp.concatenate(split(flows), axis=0))
    weights = (quads[:funds, :wide] + quads[wide : wide + funds, wide:]) + (
        quads[:funds, wide:] + quads[wide : wide + funds, :wide]
    )

    def put(values, first):
        row = first
        while row < first + values.shape[0]:
            slot, inner = row // chunk, row % chunk
            size = min(chunk - inner, first + values.shape[0] - row)
            part_buf[slot, inner : inner + size, : values.shape[1]] = values[
                row - first : row - first + size
            ]
            row += size

    put(weights, 0)
    put(classes, funds)

    pl.semaphore_wait(barrier, n - 1)

    def scatter(step):
        peer, where = peer_of(step)
        return pltpu.make_async_remote_copy(
            src_ref=part_buf.at[peer],
            dst_ref=recv_buf.at[me],
            send_sem=send_a.at[peer],
            recv_sem=recv_a.at[me],
            device_id=where,
            device_id_type=pl.DeviceIdType.MESH,
        )

    def spread(step):
        peer, where = peer_of(step)
        return pltpu.make_async_remote_copy(
            src_ref=sum_buf.at[me],
            dst_ref=sum_buf.at[me],
            send_sem=send_b.at[peer],
            recv_sem=recv_b.at[me],
            device_id=where,
            device_id_type=pl.DeviceIdType.MESH,
        )

    def arrival(buf, sems, step):
        peer, where = peer_of(step)
        return pltpu.make_async_remote_copy(
            src_ref=buf.at[peer],
            dst_ref=buf.at[peer],
            send_sem=send_a.at[peer],
            recv_sem=sems.at[peer],
            device_id=where,
            device_id_type=pl.DeviceIdType.MESH,
        )

    for step in range(1, n):
        scatter(step).start()

    for load in loads[8:]:
        load.wait()
    for k in range(kinds):
        kind_ref[k : k + 1, :] = jnp.full((1, wide), -log2_e * base_ref[k], f32)
        kind_ref[kinds + k : kinds + k + 1, :] = jnp.full((1, wide), 12.0 * sens_ref[k], f32)
        kind_ref[2 * kinds + k : 2 * kinds + k + 1, :] = jnp.exp(
            jnp.full((1, wide), -fee_ref[k], f32)
        )
    products = prod_ref[...]
    base = jnp.zeros(products.shape, f32)
    sens = base
    fee = base
    for k in range(kinds):
        match = products == k
        base = jnp.where(match, base_ref[k], base)
        sens = jnp.where(match, sens_ref[k], sens)
        fee = jnp.where(match, fee_ref[k], fee)
    rows_ref[0:1, :] = jnp.log2(worth) - (months * log2_e) * fee
    rows_ref[1:2, :] = 12.0 * sens
    for t in range(months):
        rows_ref[2 + t : 3 + t, :] = base * jnp.where(
            dur_ref[...] + t >= surrender_end, -2.0 * log2_e, -log2_e
        )

    total = part_buf[me]
    for step in range(1, n):
        arrival(recv_buf, recv_a, step).wait_recv()
        total = total + recv_buf[peer_of(step)[0]]
    sum_buf[me] = total
    for step in range(1, n):
        spread(step).start()

    tenor_years = (
        lax.broadcasted_iota(jnp.int32, (1, tenors), 1).astype(f32) + 1.0
    ) / 12.0
    disc_ref[...] = jnp.zeros_like(disc_ref)
    for t in range(months):
        rates = rates_ref[t].T
        disc_h, disc_l = split(jnp.exp(-rates * tenor_years))
        span = slice(t * scen, (t + 1) * scen)
        disc_ref[span, 0:tenors] = disc_h
        disc_ref[span, wide : wide + tenors] = disc_l
        market_ref[span, :] = jnp.broadcast_to(rates[:, tenors - 1 : tenors], (scen, wide))

    for step in range(1, n):
        arrival(sum_buf, recv_b, step).wait_recv()
    for slot in range(n):
        out_ref[slot * chunk : (slot + 1) * chunk, :] = sum_buf[slot]
    for step in range(1, n):
        scatter(step).wait_send()
        spread(step).wait_send()


def project_kernel(
    kinds,
    funds,
    block,
    sums_ref,
    hot_ref,
    rows,
    disc_ref,
    market_ref,
    kind_ref,
    share_ref,
    cred_ref,
    out_ref,
    table,
    assets_buf,
    credited_buf,
    gathered_even,
    gathered_odd,
    staged,
    out_sem,
):
    months = cred_ref.shape[0]
    scen = cred_ref.shape[2]
    wide = sums_ref.shape[1]
    policies = hot_ref.shape[1]

    weights = sums_ref[0:funds, :]
    if wide > funds:
        weights = jnp.concatenate([weights, jnp.zeros((wide - funds, wide), f32)], axis=0)
    weight_h, weight_l = split(weights)
    both = jnp.concatenate(
        [
            jnp.concatenate([weight_h, weight_h], axis=1),
            jnp.concatenate([weight_l, weight_l], axis=1),
        ],
        axis=0,
    )
    halves = dot_cols(disc_ref[...], both)
    assets_buf[...] = halves[:, :wide] + halves[:, wide:]

    base_rows, sens_rows, exp_fee = (
        [kind_ref[i * kinds + k : i * kinds + k + 1, :] for k in range(kinds)] for i in range(3)
    )
    start = [
        [[sums_ref[funds + u * kinds + k : funds + u * kinds + k + 1, :] for k in range(kinds)]
         for u in range(months)]
    ]
    for t in range(1, months):
        start.append([[w * e for w, e in zip(line, exp_fee)] for line in start[-1]])
    share = share_ref[...]
    if wide > funds:
        share = jnp.concatenate([share, jnp.zeros((1, wide - funds), f32)], axis=1)

    tile = min(scen, 32)
    lane = lax.broadcasted_iota(jnp.int32, (tile, wide), 1)
    for first in range(0, scen, tile):
        stays = []
        growth = None
        for t in range(months):
            span = slice(t * scen + first, t * scen + first + tile)
            liab = None
            for k in range(kinds):
                acc = start[t][months - 1][k]
                for u in range(months - 1, 0, -1):
                    early = months - 1 - u
                    if early < t:
                        acc = acc * stays[early][k]
                    acc = acc + start[t][u - 1][k]
                for early in range(t):
                    acc = acc * stays[early][k]
                liab = acc if liab is None else liab + acc
            if growth is not None:
                liab = liab * jnp.exp2(growth)
            ratio = jnp.where(lane < funds, assets_buf[span, :] / liab, 1.0)
            credited = share * jnp.log(ratio)
            credited_buf[span, :] = credited
            market = market_ref[span, :]
            scaled = (market - credited) * (log2_e / 12.0)
            high, low = split(scaled)
            table[span, 0:wide] = high
            table[span, wide : 2 * wide] = low
            moved = credited * (log2_e / 12.0)
            growth = moved if growth is None else growth + moved
            if t < months - 1:
                stays.append(
                    [
                        jnp.exp2(base_rows[k] * jnp.exp2(sens_rows[k] * scaled))
                        for k in range(kinds)
                    ]
                )
        high, low = split(growth)
        table[months * scen + first : months * scen + first + tile, 0:wide] = high
        table[months * scen + first : months * scen + first + tile, wide : 2 * wide] = low

    def fetch(idx, gathered):
        hot = hot_ref[:, idx * block : (idx + 1) * block]
        gathered[...] = dot(table[...], jnp.concatenate([hot, hot], axis=0))

    def settle(idx, gathered):
        cols = slice(idx * block, (idx + 1) * block)
        first_row = rows[0:1, cols]
        sens_row = rows[1:2, cols]
        for first in range(0, scen, tile):
            acc = first_row + gathered[months * scen + first : months * scen + first + tile, :]
            for t in range(months):
                spread = gathered[t * scen + first : t * scen + first + tile, :]
                acc = acc + rows[2 + t : 3 + t, cols] * jnp.exp2(sens_row * spread)
            staged[idx, first : first + tile, :] = jnp.exp2(acc)
        pltpu.make_async_copy(staged.at[idx], out_ref.at[:, cols], out_sem).start()

    blocks = policies // block
    fetch(0, gathered_even)
    for t in range(blocks, months):
        cred_ref[t] = credited_buf[t * scen : (t + 1) * scen, :].T[:funds]
    for idx in range(blocks):
        here, after = (gathered_odd, gathered_even) if idx % 2 else (gathered_even, gathered_odd)
        if idx + 1 < blocks:
            fetch(idx + 1, after)
        settle(idx, here)
        if idx < months:
            cred_ref[idx] = credited_buf[idx * scen : (idx + 1) * scen, :].T[:funds]
    pltpu.make_async_copy(out_ref, out_ref, out_sem).wait()


def local(
    group,
    count_init,
    value_init,
    durations,
    products,
    policy_fund,
    lapse_base,
    lapse_sens,
    fee_rate,
    fund_share,
    bond_flows,
    bond_fund,
    holdings,
    scen_rates,
):
    funds = fund_share.shape[0]
    months, tenors, scen = scen_rates.shape
    kinds = lapse_base.shape[0]
    policies = count_init.shape[0]
    n = group[0] * group[1]
    wide = round_up(max(funds, tenors), lanes)
    chunk = -(-(funds + months * kinds) // n)
    vmem = pl.BlockSpec(memory_space=pltpu.VMEM)
    count_row, value_row, dur_row, prod_row, pfund_row, bfund_row, hold_row = (
        x[None, :]
        for x in (
            count_init,
            value_init,
            durations,
            products,
            policy_fund,
            bond_fund,
            holdings,
        )
    )
    few = 24 << 20
    hbm = pl.BlockSpec(memory_space=pltpu.HBM)
    sources = (
        bfund_row,
        hold_row,
        bond_flows.T,
        pfund_row,
        count_row,
        value_row,
        dur_row,
        prod_row,
        lapse_base,
        lapse_sens,
        fee_rate,
        fund_share[None, :],
        scen_rates,
    )
    carried = pl.pallas_call(
        functools.partial(gather_kernel, group, kinds, funds),
        out_shape=(
            jax.ShapeDtypeStruct((n * chunk, wide), f32),
            jax.ShapeDtypeStruct((wide, policies), bf16),
            jax.ShapeDtypeStruct((round_up(2 + months, 8), policies), f32),
            jax.ShapeDtypeStruct((months * scen, 2 * wide), bf16),
            jax.ShapeDtypeStruct((months * scen, wide), f32),
            jax.ShapeDtypeStruct((3 * kinds, wide), f32),
            jax.ShapeDtypeStruct((1, funds), f32),
        ),
        in_specs=[hbm] * len(sources),
        out_specs=(vmem,) * 7,
        scratch_shapes=[
            *(pltpu.VMEM(x.shape, x.dtype) for x in sources[:8]),
            *(pltpu.SMEM(x.shape, x.dtype) for x in sources[8:11]),
            pltpu.VMEM(scen_rates.shape, f32),
            pltpu.SemaphoreType.DMA((len(sources),)),
            pltpu.VMEM((n, chunk, wide), f32),
            pltpu.VMEM((n, chunk, wide), f32),
            pltpu.VMEM((n, chunk, wide), f32),
            pltpu.SemaphoreType.DMA((n,)),
            pltpu.SemaphoreType.DMA((n,)),
            pltpu.SemaphoreType.DMA((n,)),
            pltpu.SemaphoreType.DMA((n,)),
        ],
        compiler_params=pltpu.CompilerParams(
            collective_id=0, has_side_effects=True, vmem_limit_bytes=few
        ),
        name="fund_sums",
    )(*(pltpu.with_memory_space_constraint(x, pltpu.HBM) for x in sources))
    block = policies // (2 * max(1, policies // 512))
    return pl.pallas_call(
        functools.partial(project_kernel, kinds, funds, block),
        out_shape=(
            jax.ShapeDtypeStruct((months, funds, scen), f32),
            jax.ShapeDtypeStruct((scen, policies), f32),
        ),
        in_specs=[vmem] * 7,
        out_specs=(vmem, pl.BlockSpec(memory_space=pl.ANY)),
        scratch_shapes=[
            pltpu.VMEM(((months + 1) * scen, 2 * wide), bf16),
            pltpu.VMEM((months * scen, wide), f32),
            pltpu.VMEM((months * scen, wide), f32),
            pltpu.VMEM(((months + 1) * scen, block), f32),
            pltpu.VMEM(((months + 1) * scen, block), f32),
            pltpu.VMEM((policies // block, scen, block), f32),
            pltpu.SemaphoreType.DMA,
        ],
        compiler_params=pltpu.CompilerParams(vmem_limit_bytes=few),
        name="project",
    )(*carried)


def solution(mesh):
    in_specs = (
        P(("pol", "fund")),
        P(("pol", "fund")),
        P(("pol", "fund")),
        P(("pol", "fund")),
        P(("pol", "fund")),
        P(),
        P(),
        P(),
        P(),
        P(("pol", "fund"), None),
        P(("pol", "fund")),
        P(("pol", "fund")),
        P(None, None, ("parts", "scen")),
    )
    out_specs = (P(None, None, ("parts", "scen")), P(("parts", "scen"), ("pol", "fund")))
    group = (mesh.shape["pol"], mesh.shape["fund"])
    return jax.shard_map(
        functools.partial(local, group),
        mesh=mesh,
        in_specs=in_specs,
        out_specs=out_specs,
        check_vma=False,
    )
```

```python
import functools

import jax
import jax.numpy as jnp
from jax import lax
from jax.experimental import pallas as pl
from jax.experimental.pallas import tpu as pltpu
from jax.sharding import PartitionSpec as P

surrender_end = 84
lanes = 128
log2_e = 1.4426950408889634
f32, bf16 = jnp.float32, jnp.bfloat16
contract_cols = (((1,), (1,)), ((), ()))


def round_up(value, unit):
    return -(-value // unit) * unit


def split(value):
    high = value.astype(bf16)
    return high, (value - high.astype(f32)).astype(bf16)


def dot(left, right):
    return jnp.dot(left, right, preferred_element_type=f32)


def dot_cols(left, right):
    return lax.dot_general(left, right, contract_cols, preferred_element_type=f32)


def onehot(ids_row, values, row_count):
    shape = (16, ids_row.shape[1])
    kind = bf16 if row_count <= 256 else f32
    ids = jnp.broadcast_to(ids_row.astype(f32), shape).astype(kind)
    rows = lax.broadcasted_iota(jnp.int32, shape, 0).astype(f32)
    values = [jnp.broadcast_to(v, shape).astype(bf16) for v in values]
    masks = [ids == (rows + float(g)).astype(kind) for g in range(0, row_count, 16)]
    zero = jnp.zeros(shape, bf16)
    return [jnp.concatenate([jnp.where(m, v, zero) for m in masks], axis=0) for v in values]


def dot_halves(left, right):
    middle = left.shape[1] // 2
    return dot_cols(left[:, :middle], right[:, :middle]) + dot_cols(
        left[:, middle:], right[:, middle:]
    )


def split_row(row):
    high = row.astype(bf16).astype(f32)
    return high, row - high


def middle(count):
    return sorted({(count - 1) // 2, count // 2})


def chunks(rows, count):
    edges = [min(rows, round_up(rows * i // count, 8)) for i in range(count + 1)]
    return [(first, after - first) for first, after in zip(edges, edges[1:])]


def gather_kernel(
    group,
    halves,
    kinds,
    funds,
    pfund_hbm,
    count_hbm,
    value_hbm,
    dur_hbm,
    prod_hbm,
    bfund_hbm,
    hold_hbm,
    flows_hbm,
    base_hbm,
    sens_hbm,
    fee_hbm,
    share_hbm,
    rates_hbm,
    out_ref,
    hot_ref,
    rows_ref,
    disc_ref,
    market_ref,
    kind_ref,
    share_ref,
    pfund_ref,
    count_ref,
    value_ref,
    dur_ref,
    prod_ref,
    bfund_ref,
    hold_ref,
    flows_ref,
    base_ref,
    sens_ref,
    fee_ref,
    rates_ref,
    in_sems,
    part_buf,
    sum_buf,
    send_a,
    recv_a,
    send_b,
    recv_b,
    *recv_bufs,
):
    pol_devs, fund_devs = group
    n = pol_devs * fund_devs
    months, tenors, scen = rates_ref.shape
    policies = pfund_ref.shape[1]
    wide = part_buf.shape[1]
    tenor_rows = flows_ref.shape[0]
    column = lax.axis_index("scen")
    half = lax.rem(column, halves)
    first_tenor = pl.multiple_of(half * (tenors - tenor_rows), 8)
    pairs = (
        (pfund_hbm, pfund_ref),
        (count_hbm, count_ref),
        (value_hbm, value_ref),
        (dur_hbm, dur_ref),
        (prod_hbm, prod_ref),
        (bfund_hbm, bfund_ref),
        (hold_hbm, hold_ref),
        (flows_hbm.at[pl.ds(first_tenor, tenor_rows)], flows_ref),
        (base_hbm, base_ref),
        (sens_hbm, sens_ref),
        (fee_hbm, fee_ref),
        (share_hbm, share_ref),
        (rates_hbm, rates_ref),
    )
    loads = [
        pltpu.make_async_copy(src, dst, in_sems.at[i]) for i, (src, dst) in enumerate(pairs)
    ]
    for load in loads:
        load.start()

    me = lax.axis_index("pol") * fund_devs + lax.axis_index("fund")
    last = fund_devs - 1
    owners = middle(pol_devs)
    spots = [z * fund_devs + last for z in owners]
    owned = [me == spot for spot in spots]
    owning = functools.reduce(jnp.logical_or, owned)
    bounds = chunks(part_buf.shape[0], len(owners))

    def device(z, c, other=None):
        where = {"pol": jnp.int32(z), "fund": jnp.int32(c)}
        if other is not None:
            where["scen"] = column - half + other
        return where

    barrier = pltpu.get_barrier_semaphore()

    def greet(*place):
        pl.semaphore_signal(
            barrier, inc=1, device_id=device(*place), device_id_type=pl.DeviceIdType.MESH
        )

    for other in range(halves):
        for k, z in enumerate(owners):
            pl.when(jnp.logical_not(owned[k] & (half == other)))(
                functools.partial(greet, z, last, other)
            )

    @pl.when(owning)
    def _():
        for z in range(pol_devs):
            for c in range(fund_devs):
                if z * fund_devs + c not in spots:
                    greet(z, c)

    ones = functools.partial(jnp.ones, dtype=f32)
    span = policies // halves
    here = pl.ds(pl.multiple_of(half * span, lanes), span)
    for load in loads[:5]:
        load.wait()
    worth = count_ref[:, here] * value_ref[:, here]
    late = jnp.clip(dur_ref[:, here] - (surrender_end - (months - 1)), 0, months - 1)
    kind = late * kinds + prod_ref[:, here]
    classed = jnp.concatenate(
        onehot(kind, split_row(worth), round_up(months * kinds, 16)), axis=0
    )
    (pol_hot,) = onehot(pfund_ref[:, here], [ones(worth.shape)], wide)
    sides = dot_halves(classed, pol_hot)
    middle_row = sides.shape[0] // 2
    classes = (sides[:middle_row] + sides[middle_row:])[: part_buf.shape[0] - tenor_rows]

    for load in loads[5:8]:
        load.wait()
    held = jnp.concatenate(split(flows_ref[...] * hold_ref[...]), axis=0)
    (bond_hot,) = onehot(bfund_ref[...], [ones(bfund_ref.shape)], wide)
    sides = dot_halves(held, bond_hot)
    part_buf[:tenor_rows, :] = sides[:tenor_rows] + sides[tenor_rows:]
    part_buf[tenor_rows:, :] = classes

    @pl.when(owning)
    def _():
        pl.semaphore_wait(barrier, halves * n - 1)

    @pl.when(jnp.logical_not(owning))
    def _():
        pl.semaphore_wait(barrier, len(owners))

    def collect(k):
        start, size = bounds[k]
        return pltpu.make_async_remote_copy(
            src_ref=part_buf.at[pl.ds(start, size)],
            dst_ref=recv_bufs[k].at[lax.rem(me - spots[k] + n, n)],
            send_sem=send_a.at[k],
            recv_sem=recv_a.at[k],
            device_id=device(owners[k], last),
            device_id_type=pl.DeviceIdType.MESH,
        )

    def spread(k, source, *place):
        start, size = bounds[k]
        rows = sum_buf.at[source, pl.ds(start, size)]
        return pltpu.make_async_remote_copy(
            src_ref=rows,
            dst_ref=rows,
            send_sem=send_b.at[place[2]],
            recv_sem=recv_b.at[source * len(owners) + k],
            device_id=device(*place),
            device_id_type=pl.DeviceIdType.MESH,
        )

    def many(k, first, sems, idx):
        slots = recv_bufs[k].at[pl.ds(first, n - first)]
        return pltpu.make_async_remote_copy(
            src_ref=slots,
            dst_ref=slots,
            send_sem=sems.at[idx],
            recv_sem=sems.at[idx],
            device_id=device(owners[k], last),
            device_id_type=pl.DeviceIdType.MESH,
        )

    for k in range(len(owners)):

        @pl.when(jnp.logical_not(owned[k]))
        def _(k=k):
            collect(k).start()

    (all_hot,) = onehot(pfund_ref[...], [ones(pfund_ref.shape)], wide)
    hot_ref[...] = all_hot
    for load in loads[8:]:
        load.wait()
    for k in range(kinds):
        kind_ref[k : k + 1, :] = jnp.full((1, wide), -log2_e * base_ref[k], f32)
        kind_ref[kinds + k : kinds + k + 1, :] = jnp.full((1, wide), 12.0 * sens_ref[k], f32)
        kind_ref[2 * kinds + k : 2 * kinds + k + 1, :] = jnp.exp(
            jnp.full((1, wide), -fee_ref[k], f32)
        )
    products = prod_ref[...]
    base = jnp.zeros(products.shape, f32)
    sens = base
    fee = base
    for k in range(kinds):
        match = products == k
        base = jnp.where(match, base_ref[k], base)
        sens = jnp.where(match, sens_ref[k], sens)
        fee = jnp.where(match, fee_ref[k], fee)
    rows_ref[0:1, :] = jnp.log2(count_ref[...] * value_ref[...]) - (months * log2_e) * fee
    rows_ref[1:2, :] = 12.0 * sens
    for t in range(months):
        rows_ref[2 + t : 3 + t, :] = base * jnp.where(
            dur_ref[...] + t >= surrender_end, -2.0 * log2_e, -log2_e
        )

    tenor_years = (
        lax.broadcasted_iota(jnp.int32, (1, tenors), 1).astype(f32) + 1.0
    ) / 12.0
    disc_ref[...] = jnp.zeros_like(disc_ref)
    for t in range(months):
        rates = rates_ref[t].T
        disc_h, disc_l = split(jnp.exp(-rates * tenor_years))
        rows = slice(t * scen, (t + 1) * scen)
        disc_ref[rows, 0:tenors] = disc_h
        disc_ref[rows, wide : wide + tenors] = disc_l
        market_ref[rows, :] = jnp.broadcast_to(rates[:, tenors - 1 : tenors], (scen, wide))

    for k in range(len(owners)):

        @pl.when(owned[k])
        def _(k=k):
            start, size = bounds[k]
            many(k, 1, recv_a, k).wait_recv()
            total = part_buf[start : start + size, :]
            for slot in range(1, n):
                total = total + recv_bufs[k][slot]
            sum_buf[half, start : start + size, :] = total
            for z in range(pol_devs):
                for other in range(halves):
                    for c in range(fund_devs):
                        send = spread(k, half, z, c, other)
                        if z * fund_devs + c == spots[k]:
                            pl.when(half != other)(send.start)
                        else:
                            send.start()

    for other in range(halves):
        for k in range(len(owners)):

            @pl.when(jnp.logical_not(owned[k] & (half == other)))
            def _(k=k, other=other):
                spread(k, other, owners[k], last, other).wait_recv()

    out_ref[0:tenor_rows, :] = sum_buf[0, 0:tenor_rows, :]
    if halves > 1:
        out_ref[tenor_rows:tenors, :] = sum_buf[1, 2 * tenor_rows - tenors : tenor_rows, :]
    if wide > tenors:
        out_ref[tenors:wide, :] = jnp.zeros((wide - tenors, wide), f32)
    totals = sum_buf[0, tenor_rows:, :]
    for other in range(1, halves):
        totals = totals + sum_buf[other, tenor_rows:, :]
    out_ref[wide:, :] = totals

    for k in range(len(owners)):

        @pl.when(jnp.logical_not(owned[k]))
        def _(k=k):
            collect(k).wait_send()

        @pl.when(owned[k])
        def _(k=k):
            for other in range(halves):

                @pl.when(half == other)
                def _():
                    many(k, 1, send_b, other).wait_send()

                @pl.when(half != other)
                def _():
                    many(k, 0, send_b, other).wait_send()


def project_kernel(
    kinds,
    funds,
    block,
    sums_ref,
    hot_ref,
    rows,
    disc_ref,
    market_ref,
    kind_ref,
    share_ref,
    cred_ref,
    out_ref,
    table,
    assets_buf,
    credited_buf,
    gathered_even,
    gathered_odd,
    staged,
    out_sem,
):
    months = cred_ref.shape[0]
    scen = cred_ref.shape[2]
    wide = sums_ref.shape[1]
    policies = hot_ref.shape[1]

    both = jnp.concatenate(split(sums_ref[0:wide, :]), axis=1)
    halves = dot(disc_ref[...], jnp.concatenate([both, both], axis=0))
    assets_buf[...] = halves[:, :wide] + halves[:, wide:]

    base_rows, sens_rows, exp_fee = (
        [kind_ref[i * kinds + k : i * kinds + k + 1, :] for k in range(kinds)] for i in range(3)
    )
    start = [
        [[sums_ref[wide + u * kinds + k : wide + u * kinds + k + 1, :] for k in range(kinds)]
         for u in range(months)]
    ]
    for t in range(1, months):
        start.append([[w * e for w, e in zip(line, exp_fee)] for line in start[-1]])
    share = share_ref[...]
    if wide > funds:
        share = jnp.concatenate([share, jnp.zeros((1, wide - funds), f32)], axis=1)

    tile = min(scen, 32)
    lane = lax.broadcasted_iota(jnp.int32, (tile, wide), 1)
    for first in range(0, scen, tile):
        stays = []
        growth = None
        for t in range(months):
            span = slice(t * scen + first, t * scen + first + tile)
            liab = None
            for k in range(kinds):
                acc = start[t][months - 1][k]
                for u in range(months - 1, 0, -1):
                    early = months - 1 - u
                    if early < t:
                        acc = acc * stays[early][k]
                    acc = acc + start[t][u - 1][k]
                for early in range(t):
                    acc = acc * stays[early][k]
                liab = acc if liab is None else liab + acc
            if growth is not None:
                liab = liab * jnp.exp2(growth)
            ratio = jnp.where(lane < funds, assets_buf[span, :] / liab, 1.0)
            credited = share * jnp.log(ratio)
            credited_buf[span, :] = credited
            market = market_ref[span, :]
            scaled = (market - credited) * (log2_e / 12.0)
            high, low = split(scaled)
            table[span, 0:wide] = high
            table[span, wide : 2 * wide] = low
            moved = credited * (log2_e / 12.0)
            growth = moved if growth is None else growth + moved
            if t < months - 1:
                stays.append(
                    [
                        jnp.exp2(base_rows[k] * jnp.exp2(sens_rows[k] * scaled))
                        for k in range(kinds)
                    ]
                )
        high, low = split(growth)
        table[months * scen + first : months * scen + first + tile, 0:wide] = high
        table[months * scen + first : months * scen + first + tile, wide : 2 * wide] = low

    def fetch(idx, gathered):
        hot = hot_ref[:, idx * block : (idx + 1) * block]
        gathered[...] = dot(table[...], jnp.concatenate([hot, hot], axis=0))

    def settle(idx, gathered):
        cols = slice(idx * block, (idx + 1) * block)
        first_row = rows[0:1, cols]
        sens_row = rows[1:2, cols]
        for first in range(0, scen, tile):
            acc = first_row + gathered[months * scen + first : months * scen + first + tile, :]
            for t in range(months):
                spread = gathered[t * scen + first : t * scen + first + tile, :]
                acc = acc + rows[2 + t : 3 + t, cols] * jnp.exp2(sens_row * spread)
            staged[idx, first : first + tile, :] = jnp.exp2(acc)
        pltpu.make_async_copy(staged.at[idx], out_ref.at[:, cols], out_sem).start()

    blocks = policies // block
    fetch(0, gathered_even)
    for t in range(blocks, months):
        cred_ref[t] = credited_buf[t * scen : (t + 1) * scen, :].T[:funds]
    for idx in range(blocks):
        here, after = (gathered_odd, gathered_even) if idx % 2 else (gathered_even, gathered_odd)
        if idx + 1 < blocks:
            fetch(idx + 1, after)
        settle(idx, here)
        if idx < months:
            cred_ref[idx] = credited_buf[idx * scen : (idx + 1) * scen, :].T[:funds]
    pltpu.make_async_copy(out_ref, out_ref, out_sem).wait()


def local(
    group,
    scen_devs,
    count_init,
    value_init,
    durations,
    products,
    policy_fund,
    lapse_base,
    lapse_sens,
    fee_rate,
    fund_share,
    bond_flows,
    bond_fund,
    holdings,
    scen_rates,
):
    funds = fund_share.shape[0]
    months, tenors, scen = scen_rates.shape
    kinds = lapse_base.shape[0]
    policies = count_init.shape[0]
    n = group[0] * group[1]
    wide = round_up(max(funds, tenors), lanes)
    even = scen_devs % 2 == 0 and tenors % 8 == 0 and policies % (4 * lanes) == 0
    halves = 2 if even else 1
    tenor_rows = round_up(-(-tenors // halves), 8)
    class_rows = round_up(months * kinds, 8)
    part_rows = tenor_rows + class_rows
    owners = len(middle(group[0]))
    vmem = pl.BlockSpec(memory_space=pltpu.VMEM)
    count_row, value_row, dur_row, prod_row, pfund_row, bfund_row, hold_row = (
        x[None, :]
        for x in (
            count_init,
            value_init,
            durations,
            products,
            policy_fund,
            bond_fund,
            holdings,
        )
    )
    few = 24 << 20
    hbm = pl.BlockSpec(memory_space=pltpu.HBM)
    sources = (
        pfund_row,
        count_row,
        value_row,
        dur_row,
        prod_row,
        bfund_row,
        hold_row,
        bond_flows.T,
        lapse_base,
        lapse_sens,
        fee_rate,
        fund_share[None, :],
        scen_rates,
    )
    carried = pl.pallas_call(
        functools.partial(gather_kernel, group, halves, kinds, funds),
        out_shape=(
            jax.ShapeDtypeStruct((wide + class_rows, wide), f32),
            jax.ShapeDtypeStruct((wide, policies), bf16),
            jax.ShapeDtypeStruct((round_up(2 + months, 8), policies), f32),
            jax.ShapeDtypeStruct((months * scen, 2 * wide), bf16),
            jax.ShapeDtypeStruct((months * scen, wide), f32),
            jax.ShapeDtypeStruct((3 * kinds, wide), f32),
            jax.ShapeDtypeStruct((1, funds), f32),
        ),
        in_specs=[hbm] * len(sources),
        out_specs=(vmem,) * 7,
        scratch_shapes=[
            *(pltpu.VMEM(x.shape, x.dtype) for x in sources[:7]),
            pltpu.VMEM((tenor_rows, bond_flows.shape[0]), f32),
            *(pltpu.SMEM(x.shape, x.dtype) for x in sources[8:11]),
            pltpu.VMEM(scen_rates.shape, f32),
            pltpu.SemaphoreType.DMA((len(sources),)),
            pltpu.VMEM((part_rows, wide), f32),
            pltpu.VMEM((halves, part_rows, wide), f32),
            pltpu.SemaphoreType.DMA((owners,)),
            pltpu.SemaphoreType.DMA((owners,)),
            pltpu.SemaphoreType.DMA((halves,)),
            pltpu.SemaphoreType.DMA((halves * owners,)),
            *(pltpu.VMEM((n, size, wide), f32) for _, size in chunks(part_rows, owners)),
        ],
        compiler_params=pltpu.CompilerParams(
            collective_id=0, has_side_effects=True, vmem_limit_bytes=few
        ),
        name="fund_sums",
    )(*(pltpu.with_memory_space_constraint(x, pltpu.HBM) for x in sources))
    block = policies // (2 * max(1, policies // 512))
    return pl.pallas_call(
        functools.partial(project_kernel, kinds, funds, block),
        out_shape=(
            jax.ShapeDtypeStruct((months, funds, scen), f32),
            jax.ShapeDtypeStruct((scen, policies), f32),
        ),
        in_specs=[vmem] * 7,
        out_specs=(vmem, pl.BlockSpec(memory_space=pl.ANY)),
        scratch_shapes=[
            pltpu.VMEM(((months + 1) * scen, 2 * wide), bf16),
            pltpu.VMEM((months * scen, wide), f32),
            pltpu.VMEM((months * scen, wide), f32),
            pltpu.VMEM(((months + 1) * scen, block), f32),
            pltpu.VMEM(((months + 1) * scen, block), f32),
            pltpu.VMEM((policies // block, scen, block), f32),
            pltpu.SemaphoreType.DMA,
        ],
        compiler_params=pltpu.CompilerParams(vmem_limit_bytes=few),
        name="project",
    )(*carried)


def solution(mesh):
    in_specs = (
        P(("pol", "fund")),
        P(("pol", "fund")),
        P(("pol", "fund")),
        P(("pol", "fund")),
        P(("pol", "fund")),
        P(),
        P(),
        P(),
        P(),
        P(("pol", "fund"), None),
        P(("pol", "fund")),
        P(("pol", "fund")),
        P(None, None, ("parts", "scen")),
    )
    out_specs = (P(None, None, ("parts", "scen")), P(("parts", "scen"), ("pol", "fund")))
    group = (mesh.shape["pol"], mesh.shape["fund"])
    return jax.shard_map(
        functools.partial(local, group, mesh.shape["scen"]),
        mesh=mesh,
        in_specs=in_specs,
        out_specs=out_specs,
        check_vma=False,
    )
```

```python
import functools

import jax
import jax.numpy as jnp
from jax import lax
from jax.experimental import pallas as pl
from jax.experimental.pallas import tpu as pltpu
from jax.sharding import PartitionSpec as P

surrender_end = 84
lanes = 128
log2_e = 1.4426950408889634
f32, bf16 = jnp.float32, jnp.bfloat16
contract_cols = (((1,), (1,)), ((), ()))


def round_up(value, unit):
    return -(-value // unit) * unit


def split(value):
    high = value.astype(bf16)
    return high, (value - high.astype(f32)).astype(bf16)


def dot(left, right):
    return jnp.dot(left, right, preferred_element_type=f32)


def dot_cols(left, right):
    return lax.dot_general(left, right, contract_cols, preferred_element_type=f32)


def onehot(ids_row, values, row_count):
    shape = (16, ids_row.shape[1])
    kind = bf16 if row_count <= 256 else f32
    ids = jnp.broadcast_to(ids_row.astype(f32), shape).astype(kind)
    rows = lax.broadcasted_iota(jnp.int32, shape, 0).astype(f32)
    values = [jnp.broadcast_to(v, shape).astype(bf16) for v in values]
    masks = [ids == (rows + float(g)).astype(kind) for g in range(0, row_count, 16)]
    zero = jnp.zeros(shape, bf16)
    return [jnp.concatenate([jnp.where(m, v, zero) for m in masks], axis=0) for v in values]


def dot_halves(left, right):
    middle = left.shape[1] // 2
    return dot_cols(left[:, :middle], right[:, :middle]) + dot_cols(
        left[:, middle:], right[:, middle:]
    )


def split_row(row):
    high = row.astype(bf16).astype(f32)
    return high, row - high


def middle(count):
    return sorted({(count - 1) // 2, count // 2})


def chunks(rows, count):
    edges = [min(rows, round_up(rows * i // count, 8)) for i in range(count + 1)]
    return [(first, after - first) for first, after in zip(edges, edges[1:])]


def gather_kernel(
    group,
    halves,
    kinds,
    funds,
    pfund_hbm,
    count_hbm,
    value_hbm,
    dur_hbm,
    prod_hbm,
    bfund_hbm,
    hold_hbm,
    flows_hbm,
    base_hbm,
    sens_hbm,
    fee_hbm,
    share_hbm,
    rates_hbm,
    out_ref,
    hot_ref,
    rows_ref,
    disc_ref,
    market_ref,
    kind_ref,
    share_ref,
    pfund_ref,
    count_ref,
    value_ref,
    dur_ref,
    prod_ref,
    bfund_ref,
    hold_ref,
    flows_ref,
    base_ref,
    sens_ref,
    fee_ref,
    rates_ref,
    in_sems,
    part_buf,
    sum_buf,
    send_a,
    recv_a,
    send_b,
    recv_b,
    *recv_bufs,
):
    pol_devs, fund_devs = group
    n = pol_devs * fund_devs
    months, tenors, scen = rates_ref.shape
    policies = pfund_ref.shape[1]
    wide = part_buf.shape[1]
    tenor_rows = flows_ref.shape[0]
    column = lax.axis_index("scen")
    half = lax.rem(column, halves)
    first_tenor = pl.multiple_of(half * (tenors - tenor_rows), 8)
    pairs = (
        (pfund_hbm, pfund_ref),
        (count_hbm, count_ref),
        (value_hbm, value_ref),
        (dur_hbm, dur_ref),
        (prod_hbm, prod_ref),
        (bfund_hbm, bfund_ref),
        (hold_hbm, hold_ref),
        (flows_hbm.at[pl.ds(first_tenor, tenor_rows)], flows_ref),
        (base_hbm, base_ref),
        (sens_hbm, sens_ref),
        (fee_hbm, fee_ref),
        (share_hbm, share_ref),
        (rates_hbm, rates_ref),
    )
    loads = [
        pltpu.make_async_copy(src, dst, in_sems.at[i]) for i, (src, dst) in enumerate(pairs)
    ]
    for load in loads:
        load.start()

    me = lax.axis_index("pol") * fund_devs + lax.axis_index("fund")
    last = fund_devs - 1
    owners = middle(pol_devs)
    spots = [z * fund_devs + last for z in owners]
    owned = [me == spot for spot in spots]
    owning = functools.reduce(jnp.logical_or, owned)
    bounds = chunks(part_buf.shape[0], len(owners))

    def device(z, c, other=None):
        where = {"pol": jnp.int32(z), "fund": jnp.int32(c)}
        if other is not None:
            where["scen"] = column - half + other
        return where

    barrier = pltpu.get_barrier_semaphore()

    def greet(*place):
        pl.semaphore_signal(
            barrier, inc=1, device_id=device(*place), device_id_type=pl.DeviceIdType.MESH
        )

    for other in range(halves):
        for k, z in enumerate(owners):
            pl.when(jnp.logical_not(owned[k] & (half == other)))(
                functools.partial(greet, z, last, other)
            )

    @pl.when(owning)
    def _():
        for z in range(pol_devs):
            for c in range(fund_devs):
                if z * fund_devs + c not in spots:
                    greet(z, c)

    ones = functools.partial(jnp.ones, dtype=f32)
    span = policies // halves
    here = pl.ds(pl.multiple_of(half * span, lanes), span)
    for load in loads[:5]:
        load.wait()
    worth = count_ref[:, here] * value_ref[:, here]
    late = jnp.clip(dur_ref[:, here] - (surrender_end - (months - 1)), 0, months - 1)
    kind = late * kinds + prod_ref[:, here]
    classed = jnp.concatenate(
        onehot(kind, split_row(worth), round_up(months * kinds, 16)), axis=0
    )
    (pol_hot,) = onehot(pfund_ref[:, here], [ones(worth.shape)], wide)
    sides = dot_halves(classed, pol_hot)
    middle_row = sides.shape[0] // 2
    classes = (sides[:middle_row] + sides[middle_row:])[: part_buf.shape[0] - tenor_rows]

    for load in loads[5:8]:
        load.wait()
    held = jnp.concatenate(split(flows_ref[...] * hold_ref[...]), axis=0)
    (bond_hot,) = onehot(bfund_ref[...], [ones(bfund_ref.shape)], wide)
    sides = dot_halves(held, bond_hot)
    part_buf[:tenor_rows, :] = sides[:tenor_rows] + sides[tenor_rows:]
    part_buf[tenor_rows:, :] = classes

    @pl.when(owning)
    def _():
        pl.semaphore_wait(barrier, halves * n - 1)

    @pl.when(jnp.logical_not(owning))
    def _():
        pl.semaphore_wait(barrier, len(owners))

    def collect(k):
        start, size = bounds[k]
        return pltpu.make_async_remote_copy(
            src_ref=part_buf.at[pl.ds(start, size)],
            dst_ref=recv_bufs[k].at[lax.rem(me - spots[k] + n, n)],
            send_sem=send_a.at[k],
            recv_sem=recv_a.at[k],
            device_id=device(owners[k], last),
            device_id_type=pl.DeviceIdType.MESH,
        )

    def spread(k, source, *place):
        start, size = bounds[k]
        rows = sum_buf.at[source, pl.ds(start, size)]
        return pltpu.make_async_remote_copy(
            src_ref=rows,
            dst_ref=rows,
            send_sem=send_b.at[place[2]],
            recv_sem=recv_b.at[source * len(owners) + k],
            device_id=device(*place),
            device_id_type=pl.DeviceIdType.MESH,
        )

    def many(k, first, sems, idx):
        slots = recv_bufs[k].at[pl.ds(first, n - first)]
        return pltpu.make_async_remote_copy(
            src_ref=slots,
            dst_ref=slots,
            send_sem=sems.at[idx],
            recv_sem=sems.at[idx],
            device_id=device(owners[k], last),
            device_id_type=pl.DeviceIdType.MESH,
        )

    for k in range(len(owners)):

        @pl.when(jnp.logical_not(owned[k]))
        def _(k=k):
            collect(k).start()

    (all_hot,) = onehot(pfund_ref[...], [ones(pfund_ref.shape)], wide)
    hot_ref[...] = all_hot
    for load in loads[8:]:
        load.wait()
    for k in range(kinds):
        kind_ref[k : k + 1, :] = jnp.full((1, wide), -log2_e * base_ref[k], f32)
        kind_ref[kinds + k : kinds + k + 1, :] = jnp.full((1, wide), 12.0 * sens_ref[k], f32)
        kind_ref[2 * kinds + k : 2 * kinds + k + 1, :] = jnp.exp(
            jnp.full((1, wide), -fee_ref[k], f32)
        )
    products = prod_ref[...]
    base = jnp.zeros(products.shape, f32)
    sens = base
    fee = base
    for k in range(kinds):
        match = products == k
        base = jnp.where(match, base_ref[k], base)
        sens = jnp.where(match, sens_ref[k], sens)
        fee = jnp.where(match, fee_ref[k], fee)
    rows_ref[0:1, :] = jnp.log2(count_ref[...] * value_ref[...]) - (months * log2_e) * fee
    rows_ref[1:2, :] = 12.0 * sens
    for t in range(months):
        rows_ref[2 + t : 3 + t, :] = base * jnp.where(
            dur_ref[...] + t >= surrender_end, -2.0 * log2_e, -log2_e
        )

    tenor_years = (
        lax.broadcasted_iota(jnp.int32, (1, tenors), 1).astype(f32) + 1.0
    ) / 12.0
    disc_ref[...] = jnp.zeros_like(disc_ref)
    for t in range(months):
        rates = rates_ref[t].T
        disc_h, disc_l = split(jnp.exp(-rates * tenor_years))
        rows = slice(t * scen, (t + 1) * scen)
        disc_ref[rows, 0:tenors] = disc_h
        disc_ref[rows, wide : wide + tenors] = disc_l
        market_ref[rows, :] = jnp.broadcast_to(rates[:, tenors - 1 : tenors], (scen, wide))

    for k in range(len(owners)):

        @pl.when(owned[k])
        def _(k=k):
            start, size = bounds[k]
            many(k, 1, recv_a, k).wait_recv()
            total = part_buf[start : start + size, :]
            for slot in range(1, n):
                total = total + recv_bufs[k][slot]
            sum_buf[half, start : start + size, :] = total
            for z in range(pol_devs):
                for other in range(halves):
                    for c in range(fund_devs):
                        send = spread(k, half, z, c, other)
                        if z * fund_devs + c == spots[k]:
                            pl.when(half != other)(send.start)
                        else:
                            send.start()

    for other in range(halves):
        for k in range(len(owners)):

            @pl.when(jnp.logical_not(owned[k] & (half == other)))
            def _(k=k, other=other):
                spread(k, other, owners[k], last, other).wait_recv()

    out_ref[0:tenor_rows, :] = sum_buf[0, 0:tenor_rows, :]
    if halves > 1:
        out_ref[tenor_rows:tenors, :] = sum_buf[1, 2 * tenor_rows - tenors : tenor_rows, :]
    if wide > tenors:
        out_ref[tenors:wide, :] = jnp.zeros((wide - tenors, wide), f32)
    totals = sum_buf[0, tenor_rows:, :]
    for other in range(1, halves):
        totals = totals + sum_buf[other, tenor_rows:, :]
    out_ref[wide:, :] = totals

    for k in range(len(owners)):

        @pl.when(jnp.logical_not(owned[k]))
        def _(k=k):
            collect(k).wait_send()

        @pl.when(owned[k])
        def _(k=k):
            for other in range(halves):

                @pl.when(half == other)
                def _():
                    many(k, 1, send_b, other).wait_send()

                @pl.when(half != other)
                def _():
                    many(k, 0, send_b, other).wait_send()


def project_kernel(
    kinds,
    funds,
    block,
    sums_ref,
    hot_ref,
    rows,
    disc_ref,
    market_ref,
    kind_ref,
    share_ref,
    cred_hbm,
    out_ref,
    table,
    assets_buf,
    credited_buf,
    gathered_even,
    gathered_odd,
    cred_ref,
    staged,
    out_sem,
    cred_sem,
):
    months = cred_ref.shape[0]
    scen = cred_ref.shape[2]
    wide = sums_ref.shape[1]
    policies = hot_ref.shape[1]

    both = jnp.concatenate(split(sums_ref[0:wide, :]), axis=1)
    halves = dot(disc_ref[...], jnp.concatenate([both, both], axis=0))
    assets_buf[...] = halves[:, :wide] + halves[:, wide:]

    base_rows, sens_rows, exp_fee = (
        [kind_ref[i * kinds + k : i * kinds + k + 1, :] for k in range(kinds)] for i in range(3)
    )
    start = [
        [[sums_ref[wide + u * kinds + k : wide + u * kinds + k + 1, :] for k in range(kinds)]
         for u in range(months)]
    ]
    for t in range(1, months):
        start.append([[w * e for w, e in zip(line, exp_fee)] for line in start[-1]])
    share = share_ref[...] * (1.0 / log2_e)
    if wide > funds:
        share = jnp.concatenate([share, jnp.zeros((1, wide - funds), f32)], axis=1)

    tile = min(scen, 32)
    lane = lax.broadcasted_iota(jnp.int32, (tile, wide), 1)
    for first in range(0, scen, tile):
        stays = []
        growth = None
        for t in range(months):
            span = slice(t * scen + first, t * scen + first + tile)
            liab = None
            for k in range(kinds):
                acc = start[t][months - 1][k]
                for u in range(months - 1, 0, -1):
                    early = months - 1 - u
                    if early < t:
                        acc = acc * stays[early][k]
                    acc = acc + start[t][u - 1][k]
                for early in range(t):
                    acc = acc * stays[early][k]
                liab = acc if liab is None else liab + acc
            ratio = jnp.log2(assets_buf[span, :]) - jnp.log2(liab)
            if growth is not None:
                ratio = ratio - growth
            credited = share * jnp.where(lane < funds, ratio, 0.0)
            credited_buf[span, :] = credited
            market = market_ref[span, :]
            scaled = (market - credited) * (log2_e / 12.0)
            high, low = split(scaled)
            table[span, 0:wide] = high
            table[span, wide : 2 * wide] = low
            moved = credited * (log2_e / 12.0)
            growth = moved if growth is None else growth + moved
            if t < months - 1:
                stays.append(
                    [
                        jnp.exp2(base_rows[k] * jnp.exp2(sens_rows[k] * scaled))
                        for k in range(kinds)
                    ]
                )
        high, low = split(growth)
        table[months * scen + first : months * scen + first + tile, 0:wide] = high
        table[months * scen + first : months * scen + first + tile, wide : 2 * wide] = low

    def fetch(idx, gathered):
        hot = hot_ref[:, idx * block : (idx + 1) * block]
        gathered[...] = dot(table[...], jnp.concatenate([hot, hot], axis=0))

    def settle(idx, gathered):
        cols = slice(idx * block, (idx + 1) * block)
        first_row = rows[0:1, cols]
        sens_row = rows[1:2, cols]
        for first in range(0, scen, tile):
            acc = first_row + gathered[months * scen + first : months * scen + first + tile, :]
            for t in range(months):
                spread = gathered[t * scen + first : t * scen + first + tile, :]
                acc = acc + rows[2 + t : 3 + t, cols] * jnp.exp2(sens_row * spread)
            staged[idx, first : first + tile, :] = jnp.exp2(acc)
        pltpu.make_async_copy(staged.at[idx], out_ref.at[:, cols], out_sem).start()

    credited_out = pltpu.make_async_copy(cred_ref, cred_hbm, cred_sem)
    blocks = policies // block
    fetch(0, gathered_even)
    for idx in range(blocks):
        here, after = (gathered_odd, gathered_even) if idx % 2 else (gathered_even, gathered_odd)
        if idx + 1 < blocks:
            fetch(idx + 1, after)
        settle(idx, here)
        if idx == 0:
            for t in range(months):
                cred_ref[t] = credited_buf[t * scen : (t + 1) * scen, :].T[:funds]
            credited_out.start()
    credited_out.wait()
    pltpu.make_async_copy(out_ref, out_ref, out_sem).wait()


def local(
    group,
    scen_devs,
    count_init,
    value_init,
    durations,
    products,
    policy_fund,
    lapse_base,
    lapse_sens,
    fee_rate,
    fund_share,
    bond_flows,
    bond_fund,
    holdings,
    scen_rates,
):
    funds = fund_share.shape[0]
    months, tenors, scen = scen_rates.shape
    kinds = lapse_base.shape[0]
    policies = count_init.shape[0]
    n = group[0] * group[1]
    wide = round_up(max(funds, tenors), lanes)
    even = scen_devs % 2 == 0 and tenors % 8 == 0 and policies % (4 * lanes) == 0
    halves = 2 if even else 1
    tenor_rows = round_up(-(-tenors // halves), 8)
    class_rows = round_up(months * kinds, 8)
    part_rows = tenor_rows + class_rows
    owners = len(middle(group[0]))
    vmem = pl.BlockSpec(memory_space=pltpu.VMEM)
    count_row, value_row, dur_row, prod_row, pfund_row, bfund_row, hold_row = (
        x[None, :]
        for x in (
            count_init,
            value_init,
            durations,
            products,
            policy_fund,
            bond_fund,
            holdings,
        )
    )
    few = 24 << 20
    hbm = pl.BlockSpec(memory_space=pltpu.HBM)
    sources = (
        pfund_row,
        count_row,
        value_row,
        dur_row,
        prod_row,
        bfund_row,
        hold_row,
        bond_flows.T,
        lapse_base,
        lapse_sens,
        fee_rate,
        fund_share[None, :],
        scen_rates,
    )
    carried = pl.pallas_call(
        functools.partial(gather_kernel, group, halves, kinds, funds),
        out_shape=(
            jax.ShapeDtypeStruct((wide + class_rows, wide), f32),
            jax.ShapeDtypeStruct((wide, policies), bf16),
            jax.ShapeDtypeStruct((round_up(2 + months, 8), policies), f32),
            jax.ShapeDtypeStruct((months * scen, 2 * wide), bf16),
            jax.ShapeDtypeStruct((months * scen, wide), f32),
            jax.ShapeDtypeStruct((3 * kinds, wide), f32),
            jax.ShapeDtypeStruct((1, funds), f32),
        ),
        in_specs=[hbm] * len(sources),
        out_specs=(vmem,) * 7,
        scratch_shapes=[
            *(pltpu.VMEM(x.shape, x.dtype) for x in sources[:7]),
            pltpu.VMEM((tenor_rows, bond_flows.shape[0]), f32),
            *(pltpu.SMEM(x.shape, x.dtype) for x in sources[8:11]),
            pltpu.VMEM(scen_rates.shape, f32),
            pltpu.SemaphoreType.DMA((len(sources),)),
            pltpu.VMEM((part_rows, wide), f32),
            pltpu.VMEM((halves, part_rows, wide), f32),
            pltpu.SemaphoreType.DMA((owners,)),
            pltpu.SemaphoreType.DMA((owners,)),
            pltpu.SemaphoreType.DMA((halves,)),
            pltpu.SemaphoreType.DMA((halves * owners,)),
            *(pltpu.VMEM((n, size, wide), f32) for _, size in chunks(part_rows, owners)),
        ],
        compiler_params=pltpu.CompilerParams(
            collective_id=0, has_side_effects=True, vmem_limit_bytes=few
        ),
        name="fund_sums",
    )(*(pltpu.with_memory_space_constraint(x, pltpu.HBM) for x in sources))
    block = policies // (2 * max(1, policies // 512))
    return pl.pallas_call(
        functools.partial(project_kernel, kinds, funds, block),
        out_shape=(
            jax.ShapeDtypeStruct((months, funds, scen), f32),
            jax.ShapeDtypeStruct((scen, policies), f32),
        ),
        in_specs=[vmem] * 7,
        out_specs=(pl.BlockSpec(memory_space=pl.ANY),) * 2,
        scratch_shapes=[
            pltpu.VMEM(((months + 1) * scen, 2 * wide), bf16),
            pltpu.VMEM((months * scen, wide), f32),
            pltpu.VMEM((months * scen, wide), f32),
            pltpu.VMEM(((months + 1) * scen, block), f32),
            pltpu.VMEM(((months + 1) * scen, block), f32),
            pltpu.VMEM((months, funds, scen), f32),
            pltpu.VMEM((policies // block, scen, block), f32),
            pltpu.SemaphoreType.DMA,
            pltpu.SemaphoreType.DMA,
        ],
        compiler_params=pltpu.CompilerParams(vmem_limit_bytes=few),
        name="project",
    )(*carried)


def solution(mesh):
    in_specs = (
        P(("pol", "fund")),
        P(("pol", "fund")),
        P(("pol", "fund")),
        P(("pol", "fund")),
        P(("pol", "fund")),
        P(),
        P(),
        P(),
        P(),
        P(("pol", "fund"), None),
        P(("pol", "fund")),
        P(("pol", "fund")),
        P(None, None, ("parts", "scen")),
    )
    out_specs = (P(None, None, ("parts", "scen")), P(("parts", "scen"), ("pol", "fund")))
    group = (mesh.shape["pol"], mesh.shape["fund"])
    return jax.shard_map(
        functools.partial(local, group, mesh.shape["scen"]),
        mesh=mesh,
        in_specs=in_specs,
        out_specs=out_specs,
        check_vma=False,
    )
```

```python
import functools

import jax
import jax.numpy as jnp
from jax import lax
from jax.experimental import pallas as pl
from jax.experimental.pallas import tpu as pltpu
from jax.sharding import PartitionSpec as P

surrender_end = 84
lanes = 128
log2_e = 1.4426950408889634
f32, bf16 = jnp.float32, jnp.bfloat16
contract_cols = (((1,), (1,)), ((), ()))


def round_up(value, unit):
    return -(-value // unit) * unit


def split(value):
    high = value.astype(bf16)
    return high, (value - high.astype(f32)).astype(bf16)


def dot(left, right):
    return jnp.dot(left, right, preferred_element_type=f32)


def dot_cols(left, right):
    return lax.dot_general(left, right, contract_cols, preferred_element_type=f32)


def onehot(ids_row, values, row_count):
    shape = (16, ids_row.shape[1])
    kind = bf16 if row_count <= 256 else f32
    ids = jnp.broadcast_to(ids_row.astype(f32), shape).astype(kind)
    rows = lax.broadcasted_iota(jnp.int32, shape, 0).astype(f32)
    values = [jnp.broadcast_to(v, shape).astype(bf16) for v in values]
    masks = [ids == (rows + float(g)).astype(kind) for g in range(0, row_count, 16)]
    zero = jnp.zeros(shape, bf16)
    return [jnp.concatenate([jnp.where(m, v, zero) for m in masks], axis=0) for v in values]


def dot_sides(left, right):
    sides = dot_cols(left, right)
    rows = sides.shape[0] // 2
    return sides[:rows] + sides[rows:]


def split_row(row):
    high = row.astype(bf16).astype(f32)
    return high, row - high


def pieces(pol_devs, rows, ready):
    return [((pol_devs - 1) // 2, 0, ready), (pol_devs // 2, ready, rows - ready)]


def gather_kernel(
    group,
    halves,
    trim,
    kinds,
    pfund_hbm,
    count_hbm,
    value_hbm,
    dur_hbm,
    prod_hbm,
    bfund_hbm,
    hold_hbm,
    flows_hbm,
    base_hbm,
    sens_hbm,
    fee_hbm,
    share_hbm,
    rates_hbm,
    out_ref,
    hot_ref,
    rows_ref,
    disc_ref,
    market_ref,
    kind_ref,
    share_ref,
    pfund_ref,
    count_ref,
    value_ref,
    dur_ref,
    prod_ref,
    bfund_ref,
    hold_ref,
    flows_ref,
    base_ref,
    sens_ref,
    fee_ref,
    rates_ref,
    in_sems,
    part_buf,
    sum_buf,
    send_a,
    recv_a,
    send_b,
    recv_b,
    *recv_bufs,
):
    pol_devs, fund_devs = group
    n = pol_devs * fund_devs
    months, tenors, scen = rates_ref.shape
    wide = part_buf.shape[1]
    tenor_rows = flows_ref.shape[0]
    column = lax.axis_index("scen")
    half = lax.rem(column, halves)
    first_tenor = pl.multiple_of(half * (tenors - tenor_rows), 8)
    pairs = (
        (bfund_hbm, bfund_ref),
        (hold_hbm, hold_ref),
        (flows_hbm.at[pl.ds(first_tenor, tenor_rows)], flows_ref),
        (pfund_hbm, pfund_ref),
        (count_hbm, count_ref),
        (value_hbm, value_ref),
        (dur_hbm, dur_ref),
        (prod_hbm, prod_ref),
        (base_hbm, base_ref),
        (sens_hbm, sens_ref),
        (fee_hbm, fee_ref),
        (share_hbm, share_ref),
        (rates_hbm, rates_ref),
    )
    loads = [
        pltpu.make_async_copy(src, dst, in_sems.at[i]) for i, (src, dst) in enumerate(pairs)
    ]
    for load in loads:
        load.start()

    me = lax.axis_index("pol") * fund_devs + lax.axis_index("fund")
    last = fund_devs - 1
    plan = pieces(pol_devs, sum_buf.shape[1], tenor_rows - trim)
    owners = [z for z, _, _ in plan]
    bounds = [(start, size) for _, start, size in plan]
    sites = sorted(set(owners))
    spots = [z * fund_devs + last for z in owners]
    owned = [me == spot for spot in spots]
    owning = functools.reduce(jnp.logical_or, owned)
    class_rows = part_buf.shape[0] - trim - tenor_rows
    classes = round_up(months * kinds, 8)

    def device(z, c, other=None):
        where = {"pol": jnp.int32(z), "fund": jnp.int32(c)}
        if other is not None:
            where["scen"] = column - half + other
        return where

    barrier = pltpu.get_barrier_semaphore()

    def greet(*place):
        pl.semaphore_signal(
            barrier, inc=1, device_id=device(*place), device_id_type=pl.DeviceIdType.MESH
        )

    @pl.when(owning)
    def _():
        for z in range(pol_devs):
            for c in range(fund_devs):
                if z * fund_devs + c not in spots:
                    greet(z, c)

    for other in range(halves):
        for z in sites:
            pl.when((me != z * fund_devs + last) | (half != other))(
                functools.partial(greet, z, last, other)
            )

    ones = functools.partial(jnp.ones, dtype=f32)
    first_row = (1 - half) * trim if halves > 1 else 0
    if trim:
        first_row = pl.multiple_of(first_row, 8)
    def collect(k):
        start, size = bounds[k]
        return pltpu.make_async_remote_copy(
            src_ref=part_buf.at[pl.ds(trim + start, size)],
            dst_ref=recv_bufs[k].at[lax.rem(me - spots[k] + n, n)],
            send_sem=send_a.at[k],
            recv_sem=recv_a.at[k],
            device_id=device(owners[k], last),
            device_id_type=pl.DeviceIdType.MESH,
        )

    def send_part(k):
        collect(k).start()

    def spread(k, source, *place):
        start, size = bounds[k]
        rows = sum_buf.at[source, pl.ds(start, size)]
        return pltpu.make_async_remote_copy(
            src_ref=rows,
            dst_ref=rows,
            send_sem=send_b.at[place[2] * len(owners) + k],
            recv_sem=recv_b.at[source * len(owners) + k],
            device_id=device(*place),
            device_id_type=pl.DeviceIdType.MESH,
        )

    def many(k, first, sems, idx):
        slots = recv_bufs[k].at[pl.ds(first, n - first)]
        return pltpu.make_async_remote_copy(
            src_ref=slots,
            dst_ref=slots,
            send_sem=sems.at[idx],
            recv_sem=sems.at[idx],
            device_id=device(owners[k], last),
            device_id_type=pl.DeviceIdType.MESH,
        )

    for load in loads[:3]:
        load.wait()
    held = jnp.concatenate(split(flows_ref[...] * hold_ref[...]), axis=0)
    (bond_hot,) = onehot(bfund_ref[...], [ones(bfund_ref.shape)], wide)
    part_buf[pl.ds(first_row, tenor_rows), :] = dot_sides(held, bond_hot)
    early = [k for k, (start, size) in enumerate(bounds) if start + size <= tenor_rows - trim]

    @pl.when(jnp.logical_not(owning))
    def _():
        pl.semaphore_wait(barrier, len(sites))
        for k in early:
            collect(k).start()

    for load in loads[3:8]:
        load.wait()
    worth = count_ref[...] * value_ref[...]
    late = jnp.clip(dur_ref[...] - (surrender_end - (months - 1)), 0, months - 1)
    kind = late * kinds + prod_ref[...] - half * (classes - class_rows)
    classed = jnp.concatenate(onehot(kind, split_row(worth), round_up(class_rows, 16)), axis=0)
    (pol_hot,) = onehot(pfund_ref[...], [ones(worth.shape)], wide)
    hot_ref[...] = pol_hot
    part_buf[pl.ds(first_row + tenor_rows, class_rows), :] = dot_sides(classed, pol_hot)[:class_rows]

    @pl.when(jnp.logical_not(owning))
    def _():
        for k in range(len(owners)):
            if k not in early:
                collect(k).start()

    @pl.when(owning)
    def _():
        pl.semaphore_wait(barrier, halves * n - 1)
        for k in range(len(owners)):
            pl.when(jnp.logical_not(owned[k]))(functools.partial(send_part, k))

    for load in loads[8:]:
        load.wait()
    for k in range(kinds):
        kind_ref[k : k + 1, :] = jnp.full((1, wide), -log2_e * base_ref[k], f32)
        kind_ref[kinds + k : kinds + k + 1, :] = jnp.full((1, wide), 12.0 * sens_ref[k], f32)
        kind_ref[2 * kinds + k : 2 * kinds + k + 1, :] = jnp.exp(
            jnp.full((1, wide), -fee_ref[k], f32)
        )
    products = prod_ref[...]
    base = jnp.zeros(products.shape, f32)
    sens = base
    fee = base
    for k in range(kinds):
        match = products == k
        base = jnp.where(match, base_ref[k], base)
        sens = jnp.where(match, sens_ref[k], sens)
        fee = jnp.where(match, fee_ref[k], fee)
    rows_ref[0:1, :] = jnp.log2(worth) - (months * log2_e) * fee
    rows_ref[1:2, :] = 12.0 * sens
    for t in range(months):
        rows_ref[2 + t : 3 + t, :] = base * jnp.where(
            dur_ref[...] + t >= surrender_end, -2.0 * log2_e, -log2_e
        )

    tenor_years = (
        lax.broadcasted_iota(jnp.int32, (1, tenors), 1).astype(f32) + 1.0
    ) / 12.0
    disc_ref[...] = jnp.zeros_like(disc_ref)
    for t in range(months):
        rates = rates_ref[t].T
        disc_h, disc_l = split(jnp.exp(-rates * tenor_years))
        rows = slice(t * scen, (t + 1) * scen)
        disc_ref[rows, 0:tenors] = disc_h
        disc_ref[rows, wide : wide + tenors] = disc_l
        market_ref[rows, :] = jnp.broadcast_to(rates[:, tenors - 1 : tenors], (scen, wide))

    for k in range(len(owners)):

        @pl.when(owned[k])
        def _(k=k):
            start, size = bounds[k]
            many(k, 1, recv_a, k).wait_recv()
            total = part_buf[trim + start : trim + start + size, :]
            for slot in range(1, n):
                total = total + recv_bufs[k][slot]
            sum_buf[half, start : start + size, :] = total
            for z in range(pol_devs):
                for other in range(halves):
                    for c in range(fund_devs):
                        send = spread(k, half, z, c, other)
                        if z * fund_devs + c == spots[k]:
                            pl.when(half != other)(send.start)
                        else:
                            send.start()

    for other in range(halves):
        for k in range(len(owners)):

            @pl.when(jnp.logical_not(owned[k] & (half == other)))
            def _(k=k, other=other):
                spread(k, other, owners[k], last, other).wait_recv()

    out_ref[0:tenor_rows, :] = sum_buf[0, 0:tenor_rows, :]
    if wide > tenors:
        out_ref[tenors:wide, :] = jnp.zeros((wide - tenors, wide), f32)
    if halves > 1:
        more = tenors - tenor_rows
        out_ref[tenor_rows:tenors, :] = sum_buf[1, tenor_rows - trim - more : tenor_rows - trim, :]
        more = classes - class_rows
        out_ref[wide : wide + more, :] = sum_buf[0, tenor_rows : tenor_rows + more, :]
        out_ref[wide + more :, :] = sum_buf[1, tenor_rows - trim : tenor_rows - trim + class_rows, :]
    else:
        out_ref[wide:, :] = sum_buf[0, tenor_rows:, :]

    for k in range(len(owners)):

        @pl.when(jnp.logical_not(owned[k]))
        def _(k=k):
            collect(k).wait_send()

        @pl.when(owned[k])
        def _(k=k):
            for other in range(halves):

                @pl.when(half == other)
                def _():
                    many(k, 1, send_b, other * len(owners) + k).wait_send()

                @pl.when(half != other)
                def _():
                    many(k, 0, send_b, other * len(owners) + k).wait_send()


def project_kernel(
    kinds,
    funds,
    block,
    sums_ref,
    hot_ref,
    rows,
    disc_ref,
    market_ref,
    kind_ref,
    share_ref,
    cred_hbm,
    out_ref,
    table,
    assets_buf,
    credited_buf,
    gathered_even,
    gathered_odd,
    cred_ref,
    staged,
    out_sem,
    cred_sem,
):
    months = cred_ref.shape[0]
    scen = cred_ref.shape[2]
    wide = sums_ref.shape[1]
    policies = hot_ref.shape[1]

    both = jnp.concatenate(split(sums_ref[0:wide, :]), axis=1)
    halves = dot(disc_ref[...], jnp.concatenate([both, both], axis=0))
    assets_buf[...] = halves[:, :wide] + halves[:, wide:]

    base_rows, sens_rows, exp_fee = (
        [kind_ref[i * kinds + k : i * kinds + k + 1, :] for k in range(kinds)] for i in range(3)
    )
    start = [
        [[sums_ref[wide + u * kinds + k : wide + u * kinds + k + 1, :] for k in range(kinds)]
         for u in range(months)]
    ]
    for t in range(1, months):
        start.append([[w * e for w, e in zip(line, exp_fee)] for line in start[-1]])
    share = share_ref[...] * (1.0 / log2_e)
    if wide > funds:
        share = jnp.concatenate([share, jnp.zeros((1, wide - funds), f32)], axis=1)

    tile = min(scen, 32)
    lane = lax.broadcasted_iota(jnp.int32, (tile, wide), 1)
    for first in range(0, scen, tile):
        stays = []
        growth = None
        for t in range(months):
            span = slice(t * scen + first, t * scen + first + tile)
            liab = None
            for k in range(kinds):
                acc = start[t][months - 1][k]
                for u in range(months - 1, 0, -1):
                    early = months - 1 - u
                    if early < t:
                        acc = acc * stays[early][k]
                    acc = acc + start[t][u - 1][k]
                for early in range(t):
                    acc = acc * stays[early][k]
                liab = acc if liab is None else liab + acc
            ratio = jnp.log2(assets_buf[span, :]) - jnp.log2(liab)
            if growth is not None:
                ratio = ratio - growth
            credited = share * jnp.where(lane < funds, ratio, 0.0)
            credited_buf[span, :] = credited
            market = market_ref[span, :]
            scaled = (market - credited) * (log2_e / 12.0)
            high, low = split(scaled)
            table[span, 0:wide] = high
            table[span, wide : 2 * wide] = low
            moved = credited * (log2_e / 12.0)
            growth = moved if growth is None else growth + moved
            if t < months - 1:
                stays.append(
                    [
                        jnp.exp2(base_rows[k] * jnp.exp2(sens_rows[k] * scaled))
                        for k in range(kinds)
                    ]
                )
        high, low = split(growth)
        table[months * scen + first : months * scen + first + tile, 0:wide] = high
        table[months * scen + first : months * scen + first + tile, wide : 2 * wide] = low

    def fetch(idx, gathered):
        hot = hot_ref[:, idx * block : (idx + 1) * block]
        gathered[...] = dot(table[...], jnp.concatenate([hot, hot], axis=0))

    def settle(idx, gathered):
        cols = slice(idx * block, (idx + 1) * block)
        first_row = rows[0:1, cols]
        sens_row = rows[1:2, cols]
        for first in range(0, scen, tile):
            acc = first_row + gathered[months * scen + first : months * scen + first + tile, :]
            for t in range(months):
                spread = gathered[t * scen + first : t * scen + first + tile, :]
                acc = acc + rows[2 + t : 3 + t, cols] * jnp.exp2(sens_row * spread)
            staged[idx, first : first + tile, :] = jnp.exp2(acc)
        pltpu.make_async_copy(staged.at[idx], out_ref.at[:, cols], out_sem).start()

    credited_out = pltpu.make_async_copy(cred_ref, cred_hbm, cred_sem)
    blocks = policies // block
    fetch(0, gathered_even)
    for idx in range(blocks):
        here, after = (gathered_odd, gathered_even) if idx % 2 else (gathered_even, gathered_odd)
        if idx + 1 < blocks:
            fetch(idx + 1, after)
        settle(idx, here)
        if idx == 0:
            for t in range(months):
                cred_ref[t] = credited_buf[t * scen : (t + 1) * scen, :].T[:funds]
            credited_out.start()
    credited_out.wait()
    pltpu.make_async_copy(out_ref, out_ref, out_sem).wait()


def local(
    group,
    scen_devs,
    count_init,
    value_init,
    durations,
    products,
    policy_fund,
    lapse_base,
    lapse_sens,
    fee_rate,
    fund_share,
    bond_flows,
    bond_fund,
    holdings,
    scen_rates,
):
    funds = fund_share.shape[0]
    months, tenors, scen = scen_rates.shape
    kinds = lapse_base.shape[0]
    policies = count_init.shape[0]
    n = group[0] * group[1]
    wide = round_up(max(funds, tenors), lanes)
    even = scen_devs % 2 == 0 and tenors % 8 == 0
    halves = 2 if even else 1
    tenor_rows = round_up(-(-tenors // halves), 8)
    classes = round_up(months * kinds, 8)
    class_rows = round_up(-(-classes // halves), 8)
    trim = min(halves * tenor_rows - tenors, halves * class_rows - classes) if halves > 1 else 0
    part_rows = tenor_rows + class_rows
    plan = pieces(group[0], part_rows - trim, tenor_rows - trim)
    vmem = pl.BlockSpec(memory_space=pltpu.VMEM)
    count_row, value_row, dur_row, prod_row, pfund_row, bfund_row, hold_row = (
        x[None, :]
        for x in (
            count_init,
            value_init,
            durations,
            products,
            policy_fund,
            bond_fund,
            holdings,
        )
    )
    few = 24 << 20
    hbm = pl.BlockSpec(memory_space=pltpu.HBM)
    sources = (
        pfund_row,
        count_row,
        value_row,
        dur_row,
        prod_row,
        bfund_row,
        hold_row,
        bond_flows.T,
        lapse_base,
        lapse_sens,
        fee_rate,
        fund_share[None, :],
        scen_rates,
    )
    carried = pl.pallas_call(
        functools.partial(gather_kernel, group, halves, trim, kinds),
        out_shape=(
            jax.ShapeDtypeStruct((wide + classes, wide), f32),
            jax.ShapeDtypeStruct((wide, policies), bf16),
            jax.ShapeDtypeStruct((round_up(2 + months, 8), policies), f32),
            jax.ShapeDtypeStruct((months * scen, 2 * wide), bf16),
            jax.ShapeDtypeStruct((months * scen, wide), f32),
            jax.ShapeDtypeStruct((3 * kinds, wide), f32),
            jax.ShapeDtypeStruct((1, funds), f32),
        ),
        in_specs=[hbm] * len(sources),
        out_specs=(vmem,) * 7,
        scratch_shapes=[
            *(pltpu.VMEM(x.shape, x.dtype) for x in sources[:7]),
            pltpu.VMEM((tenor_rows, bond_flows.shape[0]), f32),
            *(pltpu.SMEM(x.shape, x.dtype) for x in sources[8:11]),
            pltpu.VMEM(scen_rates.shape, f32),
            pltpu.SemaphoreType.DMA((len(sources),)),
            pltpu.VMEM((part_rows + trim, wide), f32),
            pltpu.VMEM((halves, part_rows - trim, wide), f32),
            pltpu.SemaphoreType.DMA((len(plan),)),
            pltpu.SemaphoreType.DMA((len(plan),)),
            pltpu.SemaphoreType.DMA((halves * len(plan),)),
            pltpu.SemaphoreType.DMA((halves * len(plan),)),
            *(pltpu.VMEM((n, size, wide), f32) for _, _, size in plan),
        ],
        compiler_params=pltpu.CompilerParams(
            collective_id=0, has_side_effects=True, vmem_limit_bytes=few
        ),
        name="fund_sums",
    )(*(pltpu.with_memory_space_constraint(x, pltpu.HBM) for x in sources))
    block = policies // (2 * max(1, policies // 512))
    return pl.pallas_call(
        functools.partial(project_kernel, kinds, funds, block),
        out_shape=(
            jax.ShapeDtypeStruct((months, funds, scen), f32),
            jax.ShapeDtypeStruct((scen, policies), f32),
        ),
        in_specs=[vmem] * 7,
        out_specs=(pl.BlockSpec(memory_space=pl.ANY),) * 2,
        scratch_shapes=[
            pltpu.VMEM(((months + 1) * scen, 2 * wide), bf16),
            pltpu.VMEM((months * scen, wide), f32),
            pltpu.VMEM((months * scen, wide), f32),
            pltpu.VMEM(((months + 1) * scen, block), f32),
            pltpu.VMEM(((months + 1) * scen, block), f32),
            pltpu.VMEM((months, funds, scen), f32),
            pltpu.VMEM((policies // block, scen, block), f32),
            pltpu.SemaphoreType.DMA,
            pltpu.SemaphoreType.DMA,
        ],
        compiler_params=pltpu.CompilerParams(vmem_limit_bytes=few),
        name="project",
    )(*carried)


def solution(mesh):
    in_specs = (
        P(("pol", "fund")),
        P(("pol", "fund")),
        P(("pol", "fund")),
        P(("pol", "fund")),
        P(("pol", "fund")),
        P(),
        P(),
        P(),
        P(),
        P(("pol", "fund"), None),
        P(("pol", "fund")),
        P(("pol", "fund")),
        P(None, None, ("parts", "scen")),
    )
    out_specs = (P(None, None, ("parts", "scen")), P(("parts", "scen"), ("pol", "fund")))
    group = (mesh.shape["pol"], mesh.shape["fund"])
    return jax.shard_map(
        functools.partial(local, group, mesh.shape["scen"]),
        mesh=mesh,
        in_specs=in_specs,
        out_specs=out_specs,
        check_vma=False,
    )
```

```python
import functools

import jax
import jax.numpy as jnp
from jax import lax
from jax.experimental import pallas as pl
from jax.experimental.pallas import tpu as pltpu
from jax.sharding import PartitionSpec as P

surrender_end = 84
lanes = 128
log2_e = 1.4426950408889634
f32, bf16 = jnp.float32, jnp.bfloat16
contract_cols = (((1,), (1,)), ((), ()))


def round_up(value, unit):
    return -(-value // unit) * unit


def split(value):
    high = value.astype(bf16)
    return high, (value - high.astype(f32)).astype(bf16)


def dot(left, right):
    return jnp.dot(left, right, preferred_element_type=f32)


def dot_cols(left, right):
    return lax.dot_general(left, right, contract_cols, preferred_element_type=f32)


def onehot(ids_row, values, row_count):
    shape = (16, ids_row.shape[1])
    kind = bf16 if row_count <= 256 else f32
    ids = jnp.broadcast_to(ids_row.astype(f32), shape).astype(kind)
    rows = lax.broadcasted_iota(jnp.int32, shape, 0).astype(f32)
    values = [jnp.broadcast_to(v, shape).astype(bf16) for v in values]
    masks = [ids == (rows + float(g)).astype(kind) for g in range(0, row_count, 16)]
    zero = jnp.zeros(shape, bf16)
    return [jnp.concatenate([jnp.where(m, v, zero) for m in masks], axis=0) for v in values]


def dot_sides(left, right):
    sides = dot_cols(left, right)
    rows = sides.shape[0] // 2
    return sides[:rows] + sides[rows:]


def split_row(row):
    high = row.astype(bf16).astype(f32)
    return high, row - high


def pieces(pol_devs, rows, ready):
    return [((pol_devs - 1) // 2, 0, ready), (pol_devs // 2, ready, rows - ready)]


def gather_kernel(
    group,
    halves,
    trim,
    kinds,
    pfund_hbm,
    count_hbm,
    value_hbm,
    dur_hbm,
    prod_hbm,
    bfund_hbm,
    hold_hbm,
    flows_hbm,
    base_hbm,
    sens_hbm,
    fee_hbm,
    share_hbm,
    rates_hbm,
    out_ref,
    hot_ref,
    rows_ref,
    disc_ref,
    market_ref,
    kind_ref,
    share_ref,
    pfund_ref,
    count_ref,
    value_ref,
    dur_ref,
    prod_ref,
    bfund_ref,
    hold_ref,
    flows_ref,
    base_ref,
    sens_ref,
    fee_ref,
    rates_ref,
    part_buf,
    sum_buf,
    send_a,
    recv_a,
    send_b,
    recv_b,
    *recv_bufs,
):
    pol_devs, fund_devs = group
    n = pol_devs * fund_devs
    months, tenors, scen = rates_ref.shape
    wide = part_buf.shape[1]
    tenor_rows = flows_ref.shape[0]
    column = lax.axis_index("scen")
    half = lax.rem(column, halves)
    first_tenor = pl.multiple_of(half * (tenors - tenor_rows), 8)
    pairs = (
        (bfund_hbm, bfund_ref),
        (hold_hbm, hold_ref),
        (flows_hbm.at[pl.ds(first_tenor, tenor_rows)], flows_ref),
        (pfund_hbm, pfund_ref),
        (count_hbm, count_ref),
        (value_hbm, value_ref),
        (dur_hbm, dur_ref),
        (prod_hbm, prod_ref),
        (base_hbm, base_ref),
        (sens_hbm, sens_ref),
        (fee_hbm, fee_ref),
        (share_hbm, share_ref),
        (rates_hbm, rates_ref),
    )
    me = lax.axis_index("pol") * fund_devs + lax.axis_index("fund")
    last = fund_devs - 1
    plan = pieces(pol_devs, sum_buf.shape[1], tenor_rows - trim)
    owners = [z for z, _, _ in plan]
    bounds = [(start, size) for _, start, size in plan]
    sites = sorted(set(owners))
    spots = [z * fund_devs + last for z in owners]
    owned = [me == spot for spot in spots]
    owning = functools.reduce(jnp.logical_or, owned)
    class_rows = part_buf.shape[0] - trim - tenor_rows
    classes = round_up(months * kinds, 8)

    def device(z, c, other=None):
        where = {"pol": jnp.int32(z), "fund": jnp.int32(c)}
        if other is not None:
            where["scen"] = column - half + other
        return where

    barrier = pltpu.get_barrier_semaphore()

    def greet(*place):
        pl.semaphore_signal(
            barrier, inc=1, device_id=device(*place), device_id_type=pl.DeviceIdType.MESH
        )

    def collect(k):
        start, size = bounds[k]
        return pltpu.make_async_remote_copy(
            src_ref=part_buf.at[pl.ds(trim + start, size)],
            dst_ref=recv_bufs[k].at[lax.rem(me - spots[k] + n, n)],
            send_sem=send_a.at[k],
            recv_sem=recv_a.at[k],
            device_id=device(owners[k], last),
            device_id_type=pl.DeviceIdType.MESH,
        )

    def send_part(k):
        collect(k).start()

    def spread(k, source, *place):
        start, size = bounds[k]
        rows = sum_buf.at[source, pl.ds(start, size)]
        return pltpu.make_async_remote_copy(
            src_ref=rows,
            dst_ref=rows,
            send_sem=send_b.at[place[2] * len(owners) + k],
            recv_sem=recv_b.at[source * len(owners) + k],
            device_id=device(*place),
            device_id_type=pl.DeviceIdType.MESH,
        )

    def many(k, first, sems, idx):
        slots = recv_bufs[k].at[pl.ds(first, n - first)]
        return pltpu.make_async_remote_copy(
            src_ref=slots,
            dst_ref=slots,
            send_sem=sems.at[idx],
            recv_sem=sems.at[idx],
            device_id=device(owners[k], last),
            device_id_type=pl.DeviceIdType.MESH,
        )

    def gather(in_sems):
        loads = [
            pltpu.make_async_copy(src, dst, in_sems.at[i]) for i, (src, dst) in enumerate(pairs)
        ]
        for load in loads:
            load.start()

        @pl.when(owning)
        def _():
            for z in range(pol_devs):
                for c in range(fund_devs):
                    if z * fund_devs + c not in spots:
                        greet(z, c)

        for other in range(halves):
            for z in sites:
                pl.when((me != z * fund_devs + last) | (half != other))(
                    functools.partial(greet, z, last, other)
                )

        ones = functools.partial(jnp.ones, dtype=f32)
        first_row = (1 - half) * trim if halves > 1 else 0
        if trim:
            first_row = pl.multiple_of(first_row, 8)
        for load in loads[:3]:
            load.wait()
        held = jnp.concatenate(split(flows_ref[...] * hold_ref[...]), axis=0)
        (bond_hot,) = onehot(bfund_ref[...], [ones(bfund_ref.shape)], wide)
        part_buf[pl.ds(first_row, tenor_rows), :] = dot_sides(held, bond_hot)
        early = [k for k, (start, size) in enumerate(bounds) if start + size <= tenor_rows - trim]

        @pl.when(jnp.logical_not(owning))
        def _():
            pl.semaphore_wait(barrier, len(sites))
            for k in early:
                collect(k).start()

        for load in loads[3:8]:
            load.wait()
        worth = count_ref[...] * value_ref[...]
        late = jnp.clip(dur_ref[...] - (surrender_end - (months - 1)), 0, months - 1)
        kind = late * kinds + prod_ref[...] - half * (classes - class_rows)
        classed = jnp.concatenate(onehot(kind, split_row(worth), round_up(class_rows, 16)), axis=0)
        (pol_hot,) = onehot(pfund_ref[...], [ones(worth.shape)], wide)
        hot_ref[...] = pol_hot
        part_buf[pl.ds(first_row + tenor_rows, class_rows), :] = dot_sides(classed, pol_hot)[:class_rows]

        @pl.when(jnp.logical_not(owning))
        def _():
            for k in range(len(owners)):
                if k not in early:
                    collect(k).start()

        @pl.when(owning)
        def _():
            pl.semaphore_wait(barrier, halves * n - 1)
            for k in range(len(owners)):
                pl.when(jnp.logical_not(owned[k]))(functools.partial(send_part, k))

        for load in loads[8:]:
            load.wait()
        for k in range(kinds):
            kind_ref[k : k + 1, :] = jnp.full((1, wide), -log2_e * base_ref[k], f32)
            kind_ref[kinds + k : kinds + k + 1, :] = jnp.full((1, wide), 12.0 * sens_ref[k], f32)
            kind_ref[2 * kinds + k : 2 * kinds + k + 1, :] = jnp.exp(
                jnp.full((1, wide), -fee_ref[k], f32)
            )
        products = prod_ref[...]
        base = jnp.zeros(products.shape, f32)
        sens = base
        fee = base
        for k in range(kinds):
            match = products == k
            base = jnp.where(match, base_ref[k], base)
            sens = jnp.where(match, sens_ref[k], sens)
            fee = jnp.where(match, fee_ref[k], fee)
        rows_ref[0:1, :] = jnp.log2(worth) - (months * log2_e) * fee
        rows_ref[1:2, :] = 12.0 * sens
        for t in range(months):
            rows_ref[2 + t : 3 + t, :] = base * jnp.where(
                dur_ref[...] + t >= surrender_end, -2.0 * log2_e, -log2_e
            )

        tenor_years = (
            lax.broadcasted_iota(jnp.int32, (1, tenors), 1).astype(f32) + 1.0
        ) / 12.0
        disc_ref[...] = jnp.zeros_like(disc_ref)
        for t in range(months):
            rates = rates_ref[t].T
            disc_h, disc_l = split(jnp.exp(-rates * tenor_years))
            rows = slice(t * scen, (t + 1) * scen)
            disc_ref[rows, 0:tenors] = disc_h
            disc_ref[rows, wide : wide + tenors] = disc_l
            market_ref[rows, :] = jnp.broadcast_to(rates[:, tenors - 1 : tenors], (scen, wide))

    pl.run_scoped(gather, pltpu.SemaphoreType.DMA((len(pairs),)))

    for k in range(len(owners)):

        @pl.when(owned[k])
        def _(k=k):
            start, size = bounds[k]
            many(k, 1, recv_a, k).wait_recv()
            total = part_buf[trim + start : trim + start + size, :]
            for slot in range(1, n):
                total = total + recv_bufs[k][slot]
            sum_buf[half, start : start + size, :] = total
            for z in range(pol_devs):
                for other in range(halves):
                    for c in range(fund_devs):
                        send = spread(k, half, z, c, other)
                        if z * fund_devs + c == spots[k]:
                            pl.when(half != other)(send.start)
                        else:
                            send.start()

    for other in range(halves):
        for k in range(len(owners)):

            @pl.when(jnp.logical_not(owned[k] & (half == other)))
            def _(k=k, other=other):
                spread(k, other, owners[k], last, other).wait_recv()

    out_ref[0:tenor_rows, :] = sum_buf[0, 0:tenor_rows, :]
    if wide > tenors:
        out_ref[tenors:wide, :] = jnp.zeros((wide - tenors, wide), f32)
    if halves > 1:
        more = tenors - tenor_rows
        out_ref[tenor_rows:tenors, :] = sum_buf[1, tenor_rows - trim - more : tenor_rows - trim, :]
        more = classes - class_rows
        out_ref[wide : wide + more, :] = sum_buf[0, tenor_rows : tenor_rows + more, :]
        out_ref[wide + more :, :] = sum_buf[1, tenor_rows - trim : tenor_rows - trim + class_rows, :]
    else:
        out_ref[wide:, :] = sum_buf[0, tenor_rows:, :]

    for k in range(len(owners)):

        @pl.when(jnp.logical_not(owned[k]))
        def _(k=k):
            collect(k).wait_send()

        @pl.when(owned[k])
        def _(k=k):
            for other in range(halves):

                @pl.when(half == other)
                def _():
                    many(k, 1, send_b, other * len(owners) + k).wait_send()

                @pl.when(half != other)
                def _():
                    many(k, 0, send_b, other * len(owners) + k).wait_send()


def project_kernel(
    kinds,
    funds,
    block,
    sums_ref,
    hot_ref,
    rows,
    disc_ref,
    market_ref,
    kind_ref,
    share_ref,
    cred_hbm,
    out_ref,
    table,
    assets_buf,
    credited_buf,
    gathered_even,
    gathered_odd,
    cred_ref,
    staged,
    out_sem,
    cred_sem,
):
    months = cred_ref.shape[0]
    scen = cred_ref.shape[2]
    wide = sums_ref.shape[1]
    policies = hot_ref.shape[1]

    both = jnp.concatenate(split(sums_ref[0:wide, :]), axis=1)
    halves = dot(disc_ref[...], jnp.concatenate([both, both], axis=0))
    assets_buf[...] = halves[:, :wide] + halves[:, wide:]

    base_rows, sens_rows, exp_fee = (
        [kind_ref[i * kinds + k : i * kinds + k + 1, :] for k in range(kinds)] for i in range(3)
    )
    start = [
        [[sums_ref[wide + u * kinds + k : wide + u * kinds + k + 1, :] for k in range(kinds)]
         for u in range(months)]
    ]
    for t in range(1, months):
        start.append([[w * e for w, e in zip(line, exp_fee)] for line in start[-1]])
    share = share_ref[...] * (1.0 / log2_e)
    if wide > funds:
        share = jnp.concatenate([share, jnp.zeros((1, wide - funds), f32)], axis=1)

    tile = min(scen, 16)
    lane = lax.broadcasted_iota(jnp.int32, (tile, wide), 1)
    for first in range(0, scen, tile):
        stays = []
        growth = None
        for t in range(months):
            span = slice(t * scen + first, t * scen + first + tile)
            liab = None
            for k in range(kinds):
                acc = start[t][months - 1][k]
                for u in range(months - 1, 0, -1):
                    early = months - 1 - u
                    if early < t:
                        acc = acc * stays[early][k]
                    acc = acc + start[t][u - 1][k]
                for early in range(t):
                    acc = acc * stays[early][k]
                liab = acc if liab is None else liab + acc
            ratio = jnp.log2(assets_buf[span, :]) - jnp.log2(liab)
            if growth is not None:
                ratio = ratio - growth
            credited = share * jnp.where(lane < funds, ratio, 0.0)
            credited_buf[span, :] = credited
            market = market_ref[span, :]
            scaled = (market - credited) * (log2_e / 12.0)
            high, low = split(scaled)
            table[span, 0:wide] = high
            table[span, wide : 2 * wide] = low
            moved = credited * (log2_e / 12.0)
            growth = moved if growth is None else growth + moved
            if t < months - 1:
                stays.append(
                    [
                        jnp.exp2(base_rows[k] * jnp.exp2(sens_rows[k] * scaled))
                        for k in range(kinds)
                    ]
                )
        high, low = split(growth)
        table[months * scen + first : months * scen + first + tile, 0:wide] = high
        table[months * scen + first : months * scen + first + tile, wide : 2 * wide] = low

    def fetch(idx, gathered):
        hot = hot_ref[:, idx * block : (idx + 1) * block]
        gathered[...] = dot(table[...], jnp.concatenate([hot, hot], axis=0))

    def settle(idx, gathered):
        cols = slice(idx * block, (idx + 1) * block)
        first_row = rows[0:1, cols]
        sens_row = rows[1:2, cols]
        for first in range(0, scen, tile):
            acc = first_row + gathered[months * scen + first : months * scen + first + tile, :]
            for t in range(months):
                spread = gathered[t * scen + first : t * scen + first + tile, :]
                acc = acc + rows[2 + t : 3 + t, cols] * jnp.exp2(sens_row * spread)
            staged[idx, first : first + tile, :] = jnp.exp2(acc)
        pltpu.make_async_copy(staged.at[idx], out_ref.at[:, cols], out_sem).start()

    credited_out = pltpu.make_async_copy(cred_ref, cred_hbm, cred_sem)
    blocks = policies // block
    fetch(0, gathered_even)
    for idx in range(blocks):
        here, after = (gathered_odd, gathered_even) if idx % 2 else (gathered_even, gathered_odd)
        if idx + 1 < blocks:
            fetch(idx + 1, after)
        settle(idx, here)
        if idx == 0:
            for t in range(months):
                cred_ref[t] = credited_buf[t * scen : (t + 1) * scen, :].T[:funds]
            credited_out.start()
    credited_out.wait()
    pltpu.make_async_copy(out_ref, out_ref, out_sem).wait()


def local(
    group,
    scen_devs,
    count_init,
    value_init,
    durations,
    products,
    policy_fund,
    lapse_base,
    lapse_sens,
    fee_rate,
    fund_share,
    bond_flows,
    bond_fund,
    holdings,
    scen_rates,
):
    funds = fund_share.shape[0]
    months, tenors, scen = scen_rates.shape
    kinds = lapse_base.shape[0]
    policies = count_init.shape[0]
    n = group[0] * group[1]
    wide = round_up(max(funds, tenors), lanes)
    even = scen_devs % 2 == 0 and tenors % 8 == 0
    halves = 2 if even else 1
    tenor_rows = round_up(-(-tenors // halves), 8)
    classes = round_up(months * kinds, 8)
    class_rows = round_up(-(-classes // halves), 8)
    trim = min(halves * tenor_rows - tenors, halves * class_rows - classes) if halves > 1 else 0
    part_rows = tenor_rows + class_rows
    plan = pieces(group[0], part_rows - trim, tenor_rows - trim)
    vmem = pl.BlockSpec(memory_space=pltpu.VMEM)
    count_row, value_row, dur_row, prod_row, pfund_row, bfund_row, hold_row = (
        x[None, :]
        for x in (
            count_init,
            value_init,
            durations,
            products,
            policy_fund,
            bond_fund,
            holdings,
        )
    )
    few = 24 << 20
    hbm = pl.BlockSpec(memory_space=pltpu.HBM)
    sources = (
        pfund_row,
        count_row,
        value_row,
        dur_row,
        prod_row,
        bfund_row,
        hold_row,
        bond_flows.T,
        lapse_base,
        lapse_sens,
        fee_rate,
        fund_share[None, :],
        scen_rates,
    )
    carried = pl.pallas_call(
        functools.partial(gather_kernel, group, halves, trim, kinds),
        out_shape=(
            jax.ShapeDtypeStruct((wide + classes, wide), f32),
            jax.ShapeDtypeStruct((wide, policies), bf16),
            jax.ShapeDtypeStruct((round_up(2 + months, 8), policies), f32),
            jax.ShapeDtypeStruct((months * scen, 2 * wide), bf16),
            jax.ShapeDtypeStruct((months * scen, wide), f32),
            jax.ShapeDtypeStruct((3 * kinds, wide), f32),
            jax.ShapeDtypeStruct((1, funds), f32),
        ),
        in_specs=[hbm] * len(sources),
        out_specs=(vmem,) * 7,
        scratch_shapes=[
            *(pltpu.VMEM(x.shape, x.dtype) for x in sources[:7]),
            pltpu.VMEM((tenor_rows, bond_flows.shape[0]), f32),
            *(pltpu.SMEM(x.shape, x.dtype) for x in sources[8:11]),
            pltpu.VMEM(scen_rates.shape, f32),
            pltpu.VMEM((part_rows + trim, wide), f32),
            pltpu.VMEM((halves, part_rows - trim, wide), f32),
            pltpu.SemaphoreType.DMA((len(plan),)),
            pltpu.SemaphoreType.DMA((len(plan),)),
            pltpu.SemaphoreType.DMA((halves * len(plan),)),
            pltpu.SemaphoreType.DMA((halves * len(plan),)),
            *(pltpu.VMEM((n, size, wide), f32) for _, _, size in plan),
        ],
        compiler_params=pltpu.CompilerParams(
            collective_id=0, has_side_effects=True, vmem_limit_bytes=few
        ),
        name="fund_sums",
    )(*(pltpu.with_memory_space_constraint(x, pltpu.HBM) for x in sources))
    block = policies // max(1, policies // 512)
    return pl.pallas_call(
        functools.partial(project_kernel, kinds, funds, block),
        out_shape=(
            jax.ShapeDtypeStruct((months, funds, scen), f32),
            jax.ShapeDtypeStruct((scen, policies), f32),
        ),
        in_specs=[vmem] * 7,
        out_specs=(pl.BlockSpec(memory_space=pl.ANY),) * 2,
        scratch_shapes=[
            pltpu.VMEM(((months + 1) * scen, 2 * wide), bf16),
            pltpu.VMEM((months * scen, wide), f32),
            pltpu.VMEM((months * scen, wide), f32),
            pltpu.VMEM(((months + 1) * scen, block), f32),
            pltpu.VMEM(((months + 1) * scen, block), f32),
            pltpu.VMEM((months, funds, scen), f32),
            pltpu.VMEM((policies // block, scen, block), f32),
            pltpu.SemaphoreType.DMA,
            pltpu.SemaphoreType.DMA,
        ],
        compiler_params=pltpu.CompilerParams(vmem_limit_bytes=few),
        name="project",
    )(*carried)


def solution(mesh):
    in_specs = (
        P(("pol", "fund")),
        P(("pol", "fund")),
        P(("pol", "fund")),
        P(("pol", "fund")),
        P(("pol", "fund")),
        P(),
        P(),
        P(),
        P(),
        P(("pol", "fund"), None),
        P(("pol", "fund")),
        P(("pol", "fund")),
        P(None, None, ("parts", "scen")),
    )
    out_specs = (P(None, None, ("parts", "scen")), P(("parts", "scen"), ("pol", "fund")))
    group = (mesh.shape["pol"], mesh.shape["fund"])
    return jax.shard_map(
        functools.partial(local, group, mesh.shape["scen"]),
        mesh=mesh,
        in_specs=in_specs,
        out_specs=out_specs,
        check_vma=False,
    )
```

```python
import functools

import jax
import jax.numpy as jnp
from jax import lax
from jax.experimental import pallas as pl
from jax.experimental.pallas import tpu as pltpu
from jax.sharding import PartitionSpec as P

surrender_end = 84
lanes = 128
log2_e = 1.4426950408889634
f32, bf16 = jnp.float32, jnp.bfloat16
contract_cols = (((1,), (1,)), ((), ()))


def round_up(value, unit):
    return -(-value // unit) * unit


def split(value):
    high = value.astype(bf16)
    return high, (value - high.astype(f32)).astype(bf16)


def dot(left, right):
    return jnp.dot(left, right, preferred_element_type=f32)


def dot_cols(left, right):
    return lax.dot_general(left, right, contract_cols, preferred_element_type=f32)


def onehot(ids_row, values, row_count):
    shape = (16, ids_row.shape[1])
    kind = bf16 if row_count <= 256 else f32
    ids = jnp.broadcast_to(ids_row.astype(f32), shape).astype(kind)
    rows = lax.broadcasted_iota(jnp.int32, shape, 0).astype(f32)
    values = [jnp.broadcast_to(v, shape).astype(bf16) for v in values]
    masks = [ids == (rows + float(g)).astype(kind) for g in range(0, row_count, 16)]
    zero = jnp.zeros(shape, bf16)
    return [jnp.concatenate([jnp.where(m, v, zero) for m in masks], axis=0) for v in values]


def dot_sides(left, right):
    sides = dot_cols(left, right)
    rows = sides.shape[0] // 2
    return sides[:rows] + sides[rows:]


def split_row(row):
    high = row.astype(bf16).astype(f32)
    return high, row - high


def pieces(pol_devs, rows, ready):
    return [((pol_devs - 1) // 2, 0, ready), (pol_devs // 2, ready, rows - ready)]


def gather_kernel(
    group,
    halves,
    trim,
    kinds,
    pfund_hbm,
    count_hbm,
    value_hbm,
    dur_hbm,
    prod_hbm,
    bfund_hbm,
    hold_hbm,
    flows_hbm,
    base_hbm,
    sens_hbm,
    fee_hbm,
    share_hbm,
    rates_hbm,
    out_ref,
    hot_ref,
    rows_ref,
    disc_ref,
    market_ref,
    kind_ref,
    share_ref,
    pfund_ref,
    count_ref,
    value_ref,
    dur_ref,
    prod_ref,
    bfund_ref,
    hold_ref,
    flows_ref,
    base_ref,
    sens_ref,
    fee_ref,
    rates_ref,
    part_buf,
    sum_buf,
    send_a,
    recv_a,
    send_b,
    recv_b,
    *recv_bufs,
):
    pol_devs, fund_devs = group
    n = pol_devs * fund_devs
    months, tenors, scen = rates_ref.shape
    wide = part_buf.shape[1]
    tenor_rows = flows_ref.shape[0]
    column = lax.axis_index("scen")
    half = lax.rem(column, halves)
    first_tenor = pl.multiple_of(half * (tenors - tenor_rows), 8)
    pairs = (
        (bfund_hbm, bfund_ref),
        (hold_hbm, hold_ref),
        (flows_hbm.at[pl.ds(first_tenor, tenor_rows)], flows_ref),
        (pfund_hbm, pfund_ref),
        (count_hbm, count_ref),
        (value_hbm, value_ref),
        (dur_hbm, dur_ref),
        (prod_hbm, prod_ref),
        (base_hbm, base_ref),
        (sens_hbm, sens_ref),
        (fee_hbm, fee_ref),
        (share_hbm, share_ref),
        (rates_hbm, rates_ref),
    )
    me = lax.axis_index("pol") * fund_devs + lax.axis_index("fund")
    last = fund_devs - 1
    plan = pieces(pol_devs, sum_buf.shape[1], tenor_rows - trim)
    owners = [z for z, _, _ in plan]
    bounds = [(start, size) for _, start, size in plan]
    sites = sorted(set(owners))
    spots = [z * fund_devs + last for z in owners]
    owned = [me == spot for spot in spots]
    owning = functools.reduce(jnp.logical_or, owned)
    class_rows = part_buf.shape[0] - trim - tenor_rows
    classes = round_up(months * kinds, 8)

    def device(z, c, other=None):
        where = {"pol": jnp.int32(z), "fund": jnp.int32(c)}
        if other is not None:
            where["scen"] = column - half + other
        return where

    barrier = pltpu.get_barrier_semaphore()

    def greet(*place):
        pl.semaphore_signal(
            barrier, inc=1, device_id=device(*place), device_id_type=pl.DeviceIdType.MESH
        )

    def collect(k):
        start, size = bounds[k]
        return pltpu.make_async_remote_copy(
            src_ref=part_buf.at[pl.ds(trim + start, size)],
            dst_ref=recv_bufs[k].at[lax.rem(me - spots[k] + n, n)],
            send_sem=send_a.at[k],
            recv_sem=recv_a.at[k],
            device_id=device(owners[k], last),
            device_id_type=pl.DeviceIdType.MESH,
        )

    def send_part(k):
        collect(k).start()

    def spread(k, source, *place):
        start, size = bounds[k]
        rows = sum_buf.at[source, pl.ds(start, size)]
        return pltpu.make_async_remote_copy(
            src_ref=rows,
            dst_ref=rows,
            send_sem=send_b.at[place[2] * len(owners) + k],
            recv_sem=recv_b.at[source * len(owners) + k],
            device_id=device(*place),
            device_id_type=pl.DeviceIdType.MESH,
        )

    def many(k, first, sems, idx):
        slots = recv_bufs[k].at[pl.ds(first, n - first)]
        return pltpu.make_async_remote_copy(
            src_ref=slots,
            dst_ref=slots,
            send_sem=sems.at[idx],
            recv_sem=sems.at[idx],
            device_id=device(owners[k], last),
            device_id_type=pl.DeviceIdType.MESH,
        )

    def gather(in_sems):
        loads = [
            pltpu.make_async_copy(src, dst, in_sems.at[i]) for i, (src, dst) in enumerate(pairs)
        ]
        for load in loads:
            load.start()

        @pl.when(owning)
        def _():
            for z in range(pol_devs):
                for c in range(fund_devs):
                    if z * fund_devs + c not in spots:
                        greet(z, c)

        for other in range(halves):
            for z in sites:
                pl.when((me != z * fund_devs + last) | (half != other))(
                    functools.partial(greet, z, last, other)
                )

        ones = functools.partial(jnp.ones, dtype=f32)
        first_row = (1 - half) * trim if halves > 1 else 0
        if trim:
            first_row = pl.multiple_of(first_row, 8)
        for load in loads[:3]:
            load.wait()
        held = jnp.concatenate(split(flows_ref[...] * hold_ref[...]), axis=0)
        (bond_hot,) = onehot(bfund_ref[...], [ones(bfund_ref.shape)], wide)
        part_buf[pl.ds(first_row, tenor_rows), :] = dot_sides(held, bond_hot)
        early = [k for k, (start, size) in enumerate(bounds) if start + size <= tenor_rows - trim]

        @pl.when(jnp.logical_not(owning))
        def _():
            pl.semaphore_wait(barrier, len(sites))
            for k in early:
                collect(k).start()

        for load in loads[3:8]:
            load.wait()
        worth = count_ref[...] * value_ref[...]
        late = jnp.clip(dur_ref[...] - (surrender_end - (months - 1)), 0, months - 1)
        kind = late * kinds + prod_ref[...] - half * (classes - class_rows)
        classed = jnp.concatenate(onehot(kind, split_row(worth), round_up(class_rows, 16)), axis=0)
        (pol_hot,) = onehot(pfund_ref[...], [ones(worth.shape)], wide)
        hot_ref[...] = pol_hot
        part_buf[pl.ds(first_row + tenor_rows, class_rows), :] = dot_sides(classed, pol_hot)[:class_rows]

        @pl.when(jnp.logical_not(owning))
        def _():
            for k in range(len(owners)):
                if k not in early:
                    collect(k).start()

        @pl.when(owning)
        def _():
            pl.semaphore_wait(barrier, halves * n - 1)
            for k in range(len(owners)):
                pl.when(jnp.logical_not(owned[k]))(functools.partial(send_part, k))

        for load in loads[8:]:
            load.wait()
        for k in range(kinds):
            kind_ref[k : k + 1, :] = jnp.full((1, wide), -log2_e * base_ref[k], f32)
            kind_ref[kinds + k : kinds + k + 1, :] = jnp.full((1, wide), 12.0 * sens_ref[k], f32)
            kind_ref[2 * kinds + k : 2 * kinds + k + 1, :] = jnp.exp(
                jnp.full((1, wide), -fee_ref[k], f32)
            )
        products = prod_ref[...]
        base = jnp.zeros(products.shape, f32)
        sens = base
        fee = base
        for k in range(kinds):
            match = products == k
            base = jnp.where(match, base_ref[k], base)
            sens = jnp.where(match, sens_ref[k], sens)
            fee = jnp.where(match, fee_ref[k], fee)
        rows_ref[0:1, :] = jnp.log2(worth) - (months * log2_e) * fee
        rows_ref[1:2, :] = 12.0 * sens
        for t in range(months):
            rows_ref[2 + t : 3 + t, :] = base * jnp.where(
                dur_ref[...] + t >= surrender_end, -2.0 * log2_e, -log2_e
            )

        tenor_years = (
            lax.broadcasted_iota(jnp.int32, (1, tenors), 1).astype(f32) + 1.0
        ) / 12.0
        disc_ref[...] = jnp.zeros_like(disc_ref)
        for t in range(months):
            rates = rates_ref[t].T
            disc_h, disc_l = split(jnp.exp(-rates * tenor_years))
            rows = slice(t * scen, (t + 1) * scen)
            disc_ref[rows, 0:tenors] = disc_h
            disc_ref[rows, wide : wide + tenors] = disc_l
            market_ref[rows, :] = jnp.broadcast_to(rates[:, tenors - 1 : tenors], (scen, wide))

    pl.run_scoped(gather, pltpu.SemaphoreType.DMA((len(pairs),)))

    for k in range(len(owners)):

        @pl.when(owned[k])
        def _(k=k):
            start, size = bounds[k]
            many(k, 1, recv_a, k).wait_recv()
            total = part_buf[trim + start : trim + start + size, :]
            for slot in range(1, n):
                total = total + recv_bufs[k][slot]
            sum_buf[half, start : start + size, :] = total
            for z in range(pol_devs):
                for other in range(halves):
                    for c in range(fund_devs):
                        send = spread(k, half, z, c, other)
                        if z * fund_devs + c == spots[k]:
                            pl.when(half != other)(send.start)
                        else:
                            send.start()

    for other in range(halves):
        for k in range(len(owners)):

            @pl.when(jnp.logical_not(owned[k] & (half == other)))
            def _(k=k, other=other):
                spread(k, other, owners[k], last, other).wait_recv()

    out_ref[0:tenor_rows, :] = sum_buf[0, 0:tenor_rows, :]
    if wide > tenors:
        out_ref[tenors:wide, :] = jnp.zeros((wide - tenors, wide), f32)
    if halves > 1:
        more = tenors - tenor_rows
        out_ref[tenor_rows:tenors, :] = sum_buf[1, tenor_rows - trim - more : tenor_rows - trim, :]
        more = classes - class_rows
        out_ref[wide : wide + more, :] = sum_buf[0, tenor_rows : tenor_rows + more, :]
        out_ref[wide + more :, :] = sum_buf[1, tenor_rows - trim : tenor_rows - trim + class_rows, :]
    else:
        out_ref[wide:, :] = sum_buf[0, tenor_rows:, :]

    for k in range(len(owners)):

        @pl.when(jnp.logical_not(owned[k]))
        def _(k=k):
            collect(k).wait_send()

        @pl.when(owned[k])
        def _(k=k):
            for other in range(halves):

                @pl.when(half == other)
                def _():
                    many(k, 1, send_b, other * len(owners) + k).wait_send()

                @pl.when(half != other)
                def _():
                    many(k, 0, send_b, other * len(owners) + k).wait_send()


def project_kernel(
    kinds,
    funds,
    block,
    sums_ref,
    hot_ref,
    rows,
    disc_ref,
    market_ref,
    kind_ref,
    share_ref,
    cred_hbm,
    out_ref,
    table,
    assets_buf,
    credited_buf,
    gathered_even,
    gathered_odd,
    cred_ref,
    staged,
    out_sem,
    cred_sem,
):
    months = cred_ref.shape[0]
    scen = cred_ref.shape[2]
    wide = sums_ref.shape[1]
    policies = hot_ref.shape[1]

    both = jnp.concatenate(split(sums_ref[0:wide, :]), axis=1)
    halves = dot(disc_ref[...], jnp.concatenate([both, both], axis=0))
    assets_buf[...] = halves[:, :wide] + halves[:, wide:]

    base_rows, sens_rows, exp_fee = (
        [kind_ref[i * kinds + k : i * kinds + k + 1, :] for k in range(kinds)] for i in range(3)
    )
    start = [
        [[sums_ref[wide + u * kinds + k : wide + u * kinds + k + 1, :] for k in range(kinds)]
         for u in range(months)]
    ]
    for t in range(1, months):
        start.append([[w * e for w, e in zip(line, exp_fee)] for line in start[-1]])
    share = share_ref[...] * (1.0 / log2_e)
    if wide > funds:
        share = jnp.concatenate([share, jnp.zeros((1, wide - funds), f32)], axis=1)

    tile = min(scen, 8)
    lane = lax.broadcasted_iota(jnp.int32, (tile, wide), 1)
    for first in range(0, scen, tile):
        stays = []
        growth = None
        for t in range(months):
            span = slice(t * scen + first, t * scen + first + tile)
            liab = None
            for k in range(kinds):
                acc = start[t][months - 1][k]
                for u in range(months - 1, 0, -1):
                    early = months - 1 - u
                    if early < t:
                        acc = acc * stays[early][k]
                    acc = acc + start[t][u - 1][k]
                for early in range(t):
                    acc = acc * stays[early][k]
                liab = acc if liab is None else liab + acc
            ratio = jnp.log2(assets_buf[span, :]) - jnp.log2(liab)
            if growth is not None:
                ratio = ratio - growth
            credited = share * jnp.where(lane < funds, ratio, 0.0)
            credited_buf[span, :] = credited
            market = market_ref[span, :]
            scaled = (market - credited) * (log2_e / 12.0)
            high, low = split(scaled)
            table[span, 0:wide] = high
            table[span, wide : 2 * wide] = low
            moved = credited * (log2_e / 12.0)
            growth = moved if growth is None else growth + moved
            if t < months - 1:
                stays.append(
                    [
                        jnp.exp2(base_rows[k] * jnp.exp2(sens_rows[k] * scaled))
                        for k in range(kinds)
                    ]
                )
        high, low = split(growth)
        table[months * scen + first : months * scen + first + tile, 0:wide] = high
        table[months * scen + first : months * scen + first + tile, wide : 2 * wide] = low

    def fetch(idx, gathered):
        hot = hot_ref[:, idx * block : (idx + 1) * block]
        gathered[...] = dot(table[...], jnp.concatenate([hot, hot], axis=0))

    def settle(idx, gathered):
        cols = slice(idx * block, (idx + 1) * block)
        first_row = rows[0:1, cols]
        sens_row = rows[1:2, cols]
        for first in range(0, scen, tile):
            acc = first_row + gathered[months * scen + first : months * scen + first + tile, :]
            for t in range(months):
                spread = gathered[t * scen + first : t * scen + first + tile, :]
                acc = acc + rows[2 + t : 3 + t, cols] * jnp.exp2(sens_row * spread)
            staged[idx, first : first + tile, :] = jnp.exp2(acc)
        pltpu.make_async_copy(staged.at[idx], out_ref.at[:, cols], out_sem).start()

    credited_out = pltpu.make_async_copy(cred_ref, cred_hbm, cred_sem)
    blocks = policies // block
    fetch(0, gathered_even)
    for idx in range(blocks):
        here, after = (gathered_odd, gathered_even) if idx % 2 else (gathered_even, gathered_odd)
        if idx + 1 < blocks:
            fetch(idx + 1, after)
        settle(idx, here)
        if idx == 0:
            for t in range(months):
                cred_ref[t] = credited_buf[t * scen : (t + 1) * scen, :].T[:funds]
            credited_out.start()
    credited_out.wait()
    pltpu.make_async_copy(out_ref, out_ref, out_sem).wait()


def local(
    group,
    scen_devs,
    count_init,
    value_init,
    durations,
    products,
    policy_fund,
    lapse_base,
    lapse_sens,
    fee_rate,
    fund_share,
    bond_flows,
    bond_fund,
    holdings,
    scen_rates,
):
    funds = fund_share.shape[0]
    months, tenors, scen = scen_rates.shape
    kinds = lapse_base.shape[0]
    policies = count_init.shape[0]
    n = group[0] * group[1]
    wide = round_up(max(funds, tenors), lanes)
    even = scen_devs % 2 == 0 and tenors % 8 == 0
    halves = 2 if even else 1
    tenor_rows = round_up(-(-tenors // halves), 8)
    classes = round_up(months * kinds, 8)
    class_rows = round_up(-(-classes // halves), 8)
    trim = min(halves * tenor_rows - tenors, halves * class_rows - classes) if halves > 1 else 0
    part_rows = tenor_rows + class_rows
    plan = pieces(group[0], part_rows - trim, tenor_rows - trim)
    vmem = pl.BlockSpec(memory_space=pltpu.VMEM)
    count_row, value_row, dur_row, prod_row, pfund_row, bfund_row, hold_row = (
        x[None, :]
        for x in (
            count_init,
            value_init,
            durations,
            products,
            policy_fund,
            bond_fund,
            holdings,
        )
    )
    few = 24 << 20
    hbm = pl.BlockSpec(memory_space=pltpu.HBM)
    sources = (
        pfund_row,
        count_row,
        value_row,
        dur_row,
        prod_row,
        bfund_row,
        hold_row,
        bond_flows.T,
        lapse_base,
        lapse_sens,
        fee_rate,
        fund_share[None, :],
        scen_rates,
    )
    carried = pl.pallas_call(
        functools.partial(gather_kernel, group, halves, trim, kinds),
        out_shape=(
            jax.ShapeDtypeStruct((wide + classes, wide), f32),
            jax.ShapeDtypeStruct((wide, policies), bf16),
            jax.ShapeDtypeStruct((round_up(2 + months, 8), policies), f32),
            jax.ShapeDtypeStruct((months * scen, 2 * wide), bf16),
            jax.ShapeDtypeStruct((months * scen, wide), f32),
            jax.ShapeDtypeStruct((3 * kinds, wide), f32),
            jax.ShapeDtypeStruct((1, funds), f32),
        ),
        in_specs=[hbm] * len(sources),
        out_specs=(vmem,) * 7,
        scratch_shapes=[
            *(pltpu.VMEM(x.shape, x.dtype) for x in sources[:7]),
            pltpu.VMEM((tenor_rows, bond_flows.shape[0]), f32),
            *(pltpu.SMEM(x.shape, x.dtype) for x in sources[8:11]),
            pltpu.VMEM(scen_rates.shape, f32),
            pltpu.VMEM((part_rows + trim, wide), f32),
            pltpu.VMEM((halves, part_rows - trim, wide), f32),
            pltpu.SemaphoreType.DMA((len(plan),)),
            pltpu.SemaphoreType.DMA((len(plan),)),
            pltpu.SemaphoreType.DMA((halves * len(plan),)),
            pltpu.SemaphoreType.DMA((halves * len(plan),)),
            *(pltpu.VMEM((n, size, wide), f32) for _, _, size in plan),
        ],
        compiler_params=pltpu.CompilerParams(
            collective_id=0, has_side_effects=True, vmem_limit_bytes=few
        ),
        name="fund_sums",
    )(*(pltpu.with_memory_space_constraint(x, pltpu.HBM) for x in sources))
    block = policies // max(1, policies // 512)
    return pl.pallas_call(
        functools.partial(project_kernel, kinds, funds, block),
        out_shape=(
            jax.ShapeDtypeStruct((months, funds, scen), f32),
            jax.ShapeDtypeStruct((scen, policies), f32),
        ),
        in_specs=[vmem] * 7,
        out_specs=(pl.BlockSpec(memory_space=pl.ANY),) * 2,
        scratch_shapes=[
            pltpu.VMEM(((months + 1) * scen, 2 * wide), bf16),
            pltpu.VMEM((months * scen, wide), f32),
            pltpu.VMEM((months * scen, wide), f32),
            pltpu.VMEM(((months + 1) * scen, block), f32),
            pltpu.VMEM(((months + 1) * scen, block), f32),
            pltpu.VMEM((months, funds, scen), f32),
            pltpu.VMEM((policies // block, scen, block), f32),
            pltpu.SemaphoreType.DMA,
            pltpu.SemaphoreType.DMA,
        ],
        compiler_params=pltpu.CompilerParams(vmem_limit_bytes=few),
        name="project",
    )(*carried)


def solution(mesh):
    in_specs = (
        P(("pol", "fund")),
        P(("pol", "fund")),
        P(("pol", "fund")),
        P(("pol", "fund")),
        P(("pol", "fund")),
        P(),
        P(),
        P(),
        P(),
        P(("pol", "fund"), None),
        P(("pol", "fund")),
        P(("pol", "fund")),
        P(None, None, ("parts", "scen")),
    )
    out_specs = (P(None, None, ("parts", "scen")), P(("parts", "scen"), ("pol", "fund")))
    group = (mesh.shape["pol"], mesh.shape["fund"])
    return jax.shard_map(
        functools.partial(local, group, mesh.shape["scen"]),
        mesh=mesh,
        in_specs=in_specs,
        out_specs=out_specs,
        check_vma=False,
    )
```
